32 devices in a mesh: row: 4 (over x, core), col: 8 (over z, y).
Axes of the slice: x: 2, y: 2, z: 4, core: 2. Of those that a mesh axis runs over, the one named last changes fastest.
Arguments:
- specimen: float32 [2, 1024, 2048], P(None, 'row', 'col'), may hold values from -6 to 6
- probe_field: float32 [2, 256, 256], replicated, may hold values from -5 to 5
- offsets: int32 [4, 8, 3, 2], P('row', 'col'), may hold values from -128 to 128
- amplitudes: float32 [4, 8, 3, 256, 256], P('row', 'col'), may hold values from 0.5 to 2.5
Outputs:
- updated: float32 [2, 1024, 2048], P(None, 'row', 'col')
The draws below stay inside these ranges and needn't reach their ends.
Inputs may be any that keep to these rules, and one draw needn't show every extreme that they name: Window p of tile (r, c) starts at row r * 256 + offsets[r, c, p, 0] and column c * 256 + offsets[r, c, p, 1]; windows may reach past the specimen's border, where the object is zero.
All inputs are finite; a program needn't handle non-finite values.
Results may differ from the reference program's by a relative error of at most 0.0003.
Values sent between devices are 32-bit elements; how exact they have to be, the bound alone decides.
No kernel may reach another device: no remote copies, remote signals or barrier semaphores. Data moves between devices by JAX's collectives and lax.ppermute only.
A program may use at most 64 MiB of HBM per device.

```python
import math
import jax
import jax.numpy as jnp
from jax import lax

TILE = 256
WIN = 256
HALO = 128
POS = 3
ITERS = 2
ROW_TILES = 4
COL_TILES = 8
OBJ_ROWS = 1024
OBJ_COLS = 2048


def place_ends(drawn, rng, low, largest):
    longest = drawn.shape.index(max(drawn.shape))
    spots = []
    for shift in (0, 1):
        where = [jax.random.randint(jax.random.fold_in(rng, axis), (), 0, length) for axis, length in enumerate(drawn.shape)]
        where[longest] = (where[longest] + shift) % drawn.shape[longest]
        spots.append(tuple(where))
    return drawn.at[spots[0]].set(low).at[spots[1]].set(largest)


def block_scale(rng, extent, pieces, low, top_value):
    loudness = 1.0
    for dim, parts in pieces:
        draws = jax.random.uniform(jax.random.fold_in(jax.random.fold_in(rng, 6), dim), (parts,), jnp.float32, low / len(pieces), top_value / len(pieces))
        loudness = loudness * jnp.repeat(jnp.exp(draws), extent[dim] // parts).reshape((-1,) + (1,) * (len(extent) - 1 - dim))
    return loudness


def centred(rng, extent, deviation, most, pieces=(), kind=jnp.bfloat16):
    values = jax.random.normal(rng, extent, jnp.float32) * deviation
    if len(pieces) > 0:
        values = block_scale(rng, extent, pieces, -0.22, 0.18) * values
    return jnp.clip(values, min=-most, max=most).astype(kind)


def setup_inputs(seed: int = 0) -> dict:
    key_of = jax.random.split(jax.random.key(seed), 5)
    return {
        "specimen": centred(key_of[0], (2, OBJ_ROWS, OBJ_COLS), 1.0, 6.0, ((1, 4), (2, 8)), jnp.float32),
        "probe_field": centred(key_of[1], (2, WIN, WIN), 0.7, 5.0, (), jnp.float32),
        "offsets": place_ends(jax.random.randint(key_of[2], (ROW_TILES, COL_TILES, POS, 2), 0 - HALO, TILE + HALO - WIN + 1), jax.random.fold_in(key_of[2], 1), 0 - HALO, TILE + HALO - WIN).astype(jnp.int32),
        "amplitudes": jnp.clip(0.5 + 2.0 * jax.random.uniform(key_of[3], (ROW_TILES, COL_TILES, POS, WIN, WIN), jnp.float32) ** block_scale(key_of[3], (ROW_TILES, COL_TILES, POS, WIN, WIN), ((0, 4), (1, 8)), -0.2, 0.2), 0.5, 2.5),
    }


smooth_term = 0.25
ridge_share = 0.1

def dft_tables(length):
    counter = jnp.arange(length, dtype=jnp.int32)
    product = counter[:, None] * counter[None, :] % length
    angle = product.astype(jnp.float32) * (2.0 * math.pi / length)
    scale = 1.0 / math.sqrt(length)
    return (jnp.cos(angle) * scale, -jnp.sin(angle) * scale)

def mat_left(matrix, stacked):
    return jnp.einsum('kn,pnm->pkm', matrix, stacked, precision=lax.Precision.HIGHEST)

def mat_right(stacked, matrix):
    return jnp.einsum('pnm,mk->pnk', stacked, matrix, precision=lax.Precision.HIGHEST)

def transform(cos_table, sin_table, real_part, imag_part):
    real_mid = mat_left(cos_table, real_part) - mat_left(sin_table, imag_part)
    imag_mid = mat_left(cos_table, imag_part) + mat_left(sin_table, real_part)
    real_out = mat_right(real_mid, cos_table) - mat_right(imag_mid, sin_table)
    imag_out = mat_right(imag_mid, cos_table) + mat_right(real_mid, sin_table)
    return (real_out, imag_out)

def window_gradient(probe_field, patch_real, patch_imag, amplitude, cos_table, sin_table):
    probe_real = probe_field[0]
    probe_imag = probe_field[1]
    exit_real = probe_real * patch_real - probe_imag * patch_imag
    exit_imag = probe_real * patch_imag + probe_imag * patch_real
    far_real, far_imag = transform(cos_table, sin_table, exit_real, exit_imag)
    modulus = jnp.sqrt(far_real * far_real + far_imag * far_imag + smooth_term)
    factor = 1.0 - amplitude / modulus
    back_real, back_imag = transform(cos_table, -sin_table, factor * far_real, factor * far_imag)
    grad_real = probe_real * back_real + probe_imag * back_imag
    grad_imag = probe_real * back_imag - probe_imag * back_real
    return (grad_real, grad_imag)

def reference(specimen, probe_field, offsets, amplitudes):
    cos_table, sin_table = dft_tables(WIN)
    device_count = ROW_TILES * COL_TILES
    flat_offsets = offsets.reshape(device_count, POS, 2)
    flat_amplitudes = amplitudes.reshape(device_count, POS, WIN, WIN)
    intensity = probe_field[0] * probe_field[0] + probe_field[1] * probe_field[1]
    zero_index = jnp.zeros((), jnp.int32)
    devices = jnp.arange(device_count, dtype=jnp.int32)

    def corner(device, position):
        row_block = device // COL_TILES
        col_block = device % COL_TILES
        top = (row_block * TILE + HALO + flat_offsets[device, position, 0]).astype(jnp.int32)
        left = (col_block * TILE + HALO + flat_offsets[device, position, 1]).astype(jnp.int32)
        return (top, left)

    def add_light(light, device):
        for position in range(POS):
            top, left = corner(device, position)
            block = lax.dynamic_slice(light, (top, left), (WIN, WIN))
            light = lax.dynamic_update_slice(light, block + intensity, (top, left))
        return (light, None)
    light_full = jnp.zeros((OBJ_ROWS + 2 * HALO, OBJ_COLS + 2 * HALO), jnp.float32)
    light_full, unused = lax.scan(add_light, light_full, devices)
    light_inner = light_full[HALO:HALO + OBJ_ROWS, HALO:HALO + OBJ_COLS]
    light_peak = jnp.max(light_inner)
    divisor = light_inner + ridge_share * light_peak
    padded = jnp.pad(specimen, ((0, 0), (HALO, HALO), (HALO, HALO)))
    for iteration in range(ITERS):

        def add_gradient(gradient, device):
            corners = [corner(device, position) for position in range(POS)]
            patches = jnp.stack([lax.dynamic_slice(padded, (zero_index, top, left), (2, WIN, WIN)) for top, left in corners])
            grad_real, grad_imag = window_gradient(probe_field, patches[:, 0], patches[:, 1], flat_amplitudes[device], cos_table, sin_table)
            for position in range(POS):
                top, left = corners[position]
                block = lax.dynamic_slice(gradient, (zero_index, top, left), (2, WIN, WIN))
                piece = jnp.stack([grad_real[position], grad_imag[position]])
                gradient = lax.dynamic_update_slice(gradient, block + piece, (zero_index, top, left))
            return (gradient, None)
        gradient = jnp.zeros(padded.shape, jnp.float32)
        gradient, unused = lax.scan(add_gradient, gradient, devices)
        inner = padded[:, HALO:HALO + OBJ_ROWS, HALO:HALO + OBJ_COLS] - gradient[:, HALO:HALO + OBJ_ROWS, HALO:HALO + OBJ_COLS] / divisor[None]
        padded = jnp.pad(inner, ((0, 0), (HALO, HALO), (HALO, HALO)))
    return padded[:, HALO:HALO + OBJ_ROWS, HALO:HALO + OBJ_COLS]
```

```python
import functools
import math

import jax
import jax.numpy as jnp
import numpy as np
from jax import lax
from jax.experimental import pallas as pl
from jax.experimental.pallas import tpu as pltpu
from jax.sharding import PartitionSpec as P

HALO = 128
ITERS = 2
LANES = 128

smooth_term = 0.25
ridge_share = 0.1

VM = pl.BlockSpec(memory_space=pltpu.VMEM)
SM = pl.BlockSpec(memory_space=pltpu.SMEM)
F32 = jnp.float32
BF16 = jnp.bfloat16


def shape(*dims):
    return jax.ShapeDtypeStruct(dims, F32)


def to_bf16(x):
    return np.asarray(x, np.float32).astype(BF16)


def split_table(table):
    high = to_bf16(table)
    low = to_bf16(table - high.astype(np.float64))
    return high, low


@functools.lru_cache
def dft_tables(length):
    half = length // 2
    n = np.arange(half)
    left, left_back, right, right_back = [], [], [], []
    for odd in (0, 1):
        turn = ((2 * n[:, None] + odd) * n[None, :]) % length
        angle = turn * (2.0 * math.pi / length)
        cos, sin = np.cos(angle) / math.sqrt(length), -np.sin(angle) / math.sqrt(length)
        form = np.block([[cos, -sin], [sin, cos]])
        for table, rows, columns in ((form, left, right_back), (form.T, left_back, right)):
            high, low = split_table(table)
            rows.append(np.concatenate([high, low, high], axis=1))
            columns.append(np.concatenate([high, high, low], axis=0))
    place = np.zeros((length, length), np.float32)
    place[2 * n, n] = 1.0
    place[2 * n + 1, half + n] = 1.0
    pick = to_bf16(place)
    return tuple(np.stack(t) for t in (left, left_back, right, right_back)) + (
        np.concatenate([pick, pick, pick], axis=0),
        np.concatenate([pick.T, pick.T, pick.T], axis=1),
    )


def halves(x):
    high = x.astype(BF16)
    low = (x - high.astype(F32)).astype(BF16)
    return high, low


def left_product(table, x):
    high, low = halves(x)
    return jnp.dot(
        table, jnp.concatenate([high, high, low], axis=0), preferred_element_type=F32
    )


def right_product(x, table):
    high, low = halves(x)
    return jnp.dot(
        jnp.concatenate([high, low, high], axis=1), table, preferred_element_type=F32
    )


def window_masks(offsets, position, win):
    row = offsets[0, 0, position, 0] + HALO
    column = offsets[0, 0, position, 1] + HALO
    low = lax.broadcasted_iota(jnp.int32, (win, win), 0) >= row
    near = lax.broadcasted_iota(jnp.int32, (win, win), 1) >= column
    return low, near


def roll_kernel(offsets, probe, rolled):
    win = probe.shape[1]
    for position in range(rolled.shape[0]):
        row = lax.rem(offsets[0, 0, position, 0] + HALO, win)
        column = lax.rem(offsets[0, 0, position, 1] + HALO, win)
        for plane in (0, 1):
            rolled[position, plane] = pltpu.roll(
                pltpu.roll(probe[plane], column, 1), row, 0
            )


def spread(piece, low, near, upper, lower, win, first):
    above = jnp.where(low, piece, 0.0)
    below = jnp.where(low, 0.0, piece)
    for ref, block in ((upper, above), (lower, below)):
        parts = (jnp.where(near, block, 0.0), jnp.where(near, 0.0, block))
        for lanes, part in zip((slice(0, win), slice(win, None)), parts):
            ref[:, lanes] = part if first else ref[:, lanes] + part


def gradient_kernel(
    offsets, up, top, bottom, down, probe, amplitude, left, left_back, right, right_back,
    grad_up, grad_mid, grad_down, upper, lower,
):
    count, win, _ = amplitude.shape
    half = win // 2
    edge = up.shape[1]

    def patch(plane, low, near):
        first = jnp.concatenate([up[plane], top[plane]], axis=0)
        second = jnp.concatenate([bottom[plane], down[plane]], axis=0)
        return jnp.where(
            near,
            jnp.where(low, first[:, :win], second[:, :win]),
            jnp.where(low, first[:, win:], second[:, win:]),
        )

    for position in range(count):
        low, near = window_masks(offsets, position, win)
        patch_real = patch(0, low, near)
        patch_imag = patch(1, low, near)
        probe_real, probe_imag = probe[position, 0], probe[position, 1]
        real = probe_real * patch_real - probe_imag * patch_imag
        imag = probe_real * patch_imag + probe_imag * patch_real
        summed = jnp.concatenate([real[:half] + real[half:], imag[:half] + imag[half:]], axis=0)
        differ = jnp.concatenate([real[:half] - real[half:], imag[:half] - imag[half:]], axis=0)
        even = left_product(left[0], summed)
        odd = left_product(left[1], differ)
        real = jnp.concatenate([even[:half], odd[:half]], axis=0)
        imag = jnp.concatenate([even[half:], odd[half:]], axis=0)
        summed = jnp.concatenate(
            [real[:, :half] + real[:, half:], imag[:, :half] + imag[:, half:]], axis=1
        )
        differ = jnp.concatenate(
            [real[:, :half] - real[:, half:], imag[:, :half] - imag[:, half:]], axis=1
        )
        even = right_product(summed, right[0])
        odd = right_product(differ, right[1])
        even_real, even_imag = even[:, :half], even[:, half:]
        odd_real, odd_imag = odd[:, :half], odd[:, half:]
        amp = amplitude[position]
        even_factor = 1.0 - amp[:, :half] * lax.rsqrt(
            even_real * even_real + even_imag * even_imag + smooth_term
        )
        odd_factor = 1.0 - amp[:, half:] * lax.rsqrt(
            odd_real * odd_real + odd_imag * odd_imag + smooth_term
        )
        even = jnp.concatenate([even_factor * even_real, even_factor * even_imag], axis=1)
        odd = jnp.concatenate([odd_factor * odd_real, odd_factor * odd_imag], axis=1)
        even = right_product(even, right_back[0])
        odd = right_product(odd, right_back[1])
        summed, differ = even + odd, even - odd
        real = jnp.concatenate([summed[:, :half], differ[:, :half]], axis=1)
        imag = jnp.concatenate([summed[:, half:], differ[:, half:]], axis=1)
        even = left_product(left_back[0], jnp.concatenate([real[:half], imag[:half]], axis=0))
        odd = left_product(left_back[1], jnp.concatenate([real[half:], imag[half:]], axis=0))
        summed, differ = even + odd, even - odd
        real = jnp.concatenate([summed[:half], differ[:half]], axis=0)
        imag = jnp.concatenate([summed[half:], differ[half:]], axis=0)
        for plane, piece in (
            (0, probe_real * real + probe_imag * imag),
            (1, probe_real * imag - probe_imag * real),
        ):
            spread(
                piece, low, near, upper.at[plane], lower.at[plane], win, position == 0
            )
    share(upper, lower, grad_up, grad_mid, grad_down)


def share(upper, lower, out_up, out_mid, out_down):
    edge = out_up.shape[1]
    out_up[...] = upper[:, :edge, :]
    out_mid[:, :edge, :] = upper[:, edge:, :]
    out_mid[:, edge:, :] = lower[:, :edge, :]
    out_down[...] = lower[:, edge:, :]


def light_kernel(offsets, probe, light_up, light_mid, light_down, upper, lower):
    win = probe.shape[2]
    for position in range(probe.shape[0]):
        low, near = window_masks(offsets, position, win)
        real, imag = probe[position, 0], probe[position, 1]
        spread(
            real * real + imag * imag, low, near, upper.at[0], lower.at[0], win, position == 0
        )
    share(upper, lower, light_up, light_mid, light_down)


def thirds(x):
    high = x.astype(BF16)
    rest = x - high.astype(F32)
    mid = rest.astype(BF16)
    return high, mid, (rest - mid.astype(F32)).astype(BF16)


def order_kernel(amplitude, pick, pick_back, ordered):
    for position in range(ordered.shape[0]):
        block = jnp.dot(
            pick_back[...],
            jnp.concatenate(thirds(amplitude[0, 0, position]), axis=0),
            preferred_element_type=F32,
        )
        ordered[position] = jnp.dot(
            jnp.concatenate(thirds(block), axis=1), pick[...], preferred_element_type=F32
        )


def edges_kernel(specimen, head, tail):
    head[...] = specimen[:, :, :HALO]
    tail[...] = specimen[:, :, specimen.shape[2] - HALO :]


def widen_kernel(before, specimen, after, top, bottom):
    edge = top.shape[1]
    tile = specimen.shape[2]
    for index, out in enumerate((top, bottom)):
        rows = slice(index * edge, (index + 1) * edge)
        out[:, :, :HALO] = before[:, rows, :]
        out[:, :, HALO : HALO + tile] = specimen[:, rows, :]
        out[:, :, HALO + tile :] = after[:, rows, :]


def fold_rows(mid, from_above, from_below):
    edge = from_above.shape[1]
    upper = mid[:, :edge, :] + from_above[...]
    lower = mid[:, edge:, :] + from_below[...]
    return upper, lower


def fold_strips_kernel(mid, from_above, from_below, head, tail):
    edge = from_above.shape[1]
    half = head.shape[2]
    for rows, block in zip((slice(0, edge), slice(edge, None)), fold_rows(mid, from_above, from_below)):
        head[:, rows, :] = block[:, :, :half]
        tail[:, rows, :] = block[:, :, half:]


def fold_bands_kernel(mid, from_above, from_below, head, core, tail):
    edge = from_above.shape[1]
    tile = core.shape[2]
    for rows, block in zip((slice(0, edge), slice(edge, None)), fold_rows(mid, from_above, from_below)):
        head[:, rows, :] = block[:, :, :HALO]
        core[:, rows, :] = block[:, :, HALO : HALO + tile]
        tail[:, rows, :] = block[:, :, HALO + tile :]


def light_sum_kernel(head, tail, from_left, from_right, light, largest):
    left = head[0] + from_left[0]
    right = tail[0] + from_right[0]
    half = left.shape[1]
    light[:, :half] = left
    light[:, half:] = right
    best = jnp.maximum(left[:, HALO:], right[:, : half - HALO])
    rows, columns = best.shape
    found = best[:8]
    for row in range(8, rows, 8):
        found = jnp.maximum(found, best[row : row + 8])
    top = found[:, :LANES]
    for column in range(LANES, columns, LANES):
        top = jnp.maximum(top, found[:, column : column + LANES])
    largest[...] = top


def divisor_of(light, peak):
    return light + ridge_share * jnp.max(peak[...])


def update_kernel(
    place, head, tail, from_left, from_right, light, peak, old_top, old_bottom, top, bottom
):
    edge = top.shape[1]
    half = head.shape[2]
    most = ridge_share * jnp.max(peak[...])
    has_left, has_right = place[0] > 0, place[1] > 0
    lane = lax.broadcasted_iota(jnp.int32, (edge, half), 1)
    keep_left = jnp.logical_or(lane >= HALO, has_left)
    keep_right = jnp.logical_or(lane < half - HALO, has_right)
    for index, (old, out) in enumerate(((old_top, top), (old_bottom, bottom))):
        rows = slice(index * edge, (index + 1) * edge)
        for side, (own, sent, keep) in enumerate(
            ((head, from_left, keep_left), (tail, from_right, keep_right))
        ):
            lanes = slice(side * half, (side + 1) * half)
            scale = 1.0 / (light[rows, lanes] + most)
            for plane in (0, 1):
                gradient = own[plane, rows, :] + sent[plane, rows, :]
                new = old[plane, :, lanes] - gradient * scale
                out[plane, :, lanes] = jnp.where(keep, new, 0.0)


def finish_kernel(core, from_left, from_right, light, peak, old_top, old_bottom, out):
    edge = old_top.shape[1]
    tile = out.shape[2]
    inner = slice(HALO, HALO + tile)
    most = ridge_share * jnp.max(peak[...])
    for index, old in enumerate((old_top, old_bottom)):
        rows = slice(index * edge, (index + 1) * edge)
        scale = 1.0 / (light[rows, inner] + most)
        for plane in (0, 1):
            gradient = core[plane, rows, :]
            gradient = jnp.concatenate(
                [
                    gradient[:, :HALO] + from_left[plane, rows, :],
                    gradient[:, HALO : tile - HALO],
                    gradient[:, tile - HALO :] + from_right[plane, rows, :],
                ],
                axis=1,
            ) if tile > 2 * HALO else jnp.concatenate(
                [
                    gradient[:, :HALO] + from_left[plane, rows, :],
                    gradient[:, HALO:] + from_right[plane, rows, :],
                ],
                axis=1,
            )
            out[plane, rows, :] = old[plane, :, inner] - gradient * scale


def kernel_call(body, outs, specs, name, flops=0, scratch=()):
    moved = 4 * sum(math.prod(out.shape) for out in outs)
    single = len(outs) == 1
    return pl.pallas_call(
        body,
        out_shape=outs[0] if single else outs,
        in_specs=specs,
        out_specs=VM if single else (VM,) * len(outs),
        scratch_shapes=list(scratch),
        compiler_params=pltpu.CompilerParams(vmem_limit_bytes=48 * 1024 * 1024),
        cost_estimate=pl.CostEstimate(
            flops=flops, bytes_accessed=3 * moved, transcendentals=0
        ),
        name=name,
    )


def shifted(block, axis, distance):
    count = lax.axis_size(axis)
    route = [(i - distance, i) for i in range(count) if 0 <= i - distance < count]
    return lax.ppermute(block, axis, route)


def largest_of(block, axis):
    count = lax.axis_size(axis)
    reach = 1
    while reach < count:
        route = [(i, (i + reach) % count) for i in range(count)]
        block = jnp.maximum(block, lax.ppermute(block, axis, route))
        reach *= 2
    return block


def local(specimen, probe_field, offsets, amplitudes):
    tile = specimen.shape[1]
    win = probe_field.shape[1]
    span = tile + 2 * HALO
    half = span // 2
    count = offsets.shape[2]
    left, left_back, right, right_back, pick, pick_back = [
        jnp.asarray(t) for t in dft_tables(win)
    ]
    col, cols = lax.axis_index("col"), lax.axis_size("col")
    place = jnp.stack([col > 0, col < cols - 1]).astype(jnp.int32)

    head, tail = kernel_call(
        edges_kernel, [shape(2, tile, HALO)] * 2, [VM], "edges"
    )(specimen)
    before = shifted(tail, "col", 1)
    after = shifted(head, "col", -1)

    probes = kernel_call(roll_kernel, [shape(count, 2, win, win)], [SM, VM], "roll")(
        offsets, probe_field
    )
    band, middle = shape(1, HALO, span), shape(1, tile, span)
    light_up, light_mid, light_down = kernel_call(
        light_kernel,
        [band, middle, band],
        [SM, VM],
        "light",
        scratch=[pltpu.VMEM((1, win, span), F32)] * 2,
    )(offsets, probes)
    light_above = shifted(light_down, "row", 1)
    light_below = shifted(light_up, "row", -1)
    ordered = kernel_call(order_kernel, [shape(count, win, win)], [VM] * 3, "order")(
        amplitudes, pick, pick_back
    )

    top, bottom = kernel_call(
        widen_kernel, [shape(2, tile // 2, span)] * 2, [VM] * 3, "widen"
    )(before, specimen, after)
    above = shifted(bottom, "row", 1)
    below = shifted(top, "row", -1)

    light_head, light_tail = kernel_call(
        fold_strips_kernel, [shape(1, tile, half)] * 2, [VM] * 3, "light_fold"
    )(light_mid, light_above, light_below)
    light_left = shifted(light_tail, "col", 1)
    light_right = shifted(light_head, "col", -1)

    light, peak = None, None
    for iteration in range(ITERS):
        grad_up, grad_mid, grad_down = kernel_call(
            gradient_kernel,
            [shape(2, HALO, span), shape(2, tile, span), shape(2, HALO, span)],
            [SM] + [VM] * 10,
            "gradient",
            flops=count * 8 * 2 * win * 3 * win * win,
            scratch=[pltpu.VMEM((2, win, span), F32)] * 2,
        )(
            offsets, above, top, bottom, below, probes, ordered,
            left, left_back, right, right_back,
        )
        grad_above = shifted(grad_down, "row", 1)
        grad_below = shifted(grad_up, "row", -1)
        if iteration == 0:
            light, found = kernel_call(
                light_sum_kernel, [shape(tile, span), shape(8, LANES)], [VM] * 4, "light_sum"
            )(light_head, light_tail, light_left, light_right)
            peak = largest_of(largest_of(found, "row"), "col")
        if iteration + 1 < ITERS:
            grad_head, grad_tail = kernel_call(
                fold_strips_kernel, [shape(2, tile, half)] * 2, [VM] * 3, "fold"
            )(grad_mid, grad_above, grad_below)
            from_left = shifted(grad_tail, "col", 1)
            from_right = shifted(grad_head, "col", -1)
            top, bottom = kernel_call(
                update_kernel,
                [shape(2, tile // 2, span)] * 2,
                [SM] + [VM] * 8,
                "update",
            )(place, grad_head, grad_tail, from_left, from_right, light, peak, top, bottom)
            above = shifted(bottom, "row", 1)
            below = shifted(top, "row", -1)
        else:
            head, core, tail = kernel_call(
                fold_bands_kernel,
                [shape(2, tile, HALO), shape(2, tile, tile), shape(2, tile, HALO)],
                [VM] * 3,
                "fold_last",
            )(grad_mid, grad_above, grad_below)
            from_left = shifted(tail, "col", 1)
            from_right = shifted(head, "col", -1)
            return kernel_call(
                finish_kernel, [shape(2, tile, tile)], [VM] * 7, "finish"
            )(core, from_left, from_right, light, peak, top, bottom)


def solution(mesh):
    return jax.shard_map(
        local,
        mesh=mesh,
        in_specs=(
            P(None, "row", "col"),
            P(),
            P("row", "col", None, None),
            P("row", "col", None, None, None),
        ),
        out_specs=P(None, "row", "col"),
        check_vma=False,
    )
```

```python
import functools
import math

import jax
import jax.numpy as jnp
import numpy as np
from jax import lax
from jax.experimental import pallas as pl
from jax.experimental.pallas import tpu as pltpu
from jax.sharding import PartitionSpec as P


HALO = 128
ITERS = 2
LANES = 128

smooth_term = 0.25
ridge_share = 0.1

VM = pl.BlockSpec(memory_space=pltpu.VMEM)
SM = pl.BlockSpec(memory_space=pltpu.SMEM)
F32 = jnp.float32
BF16 = jnp.bfloat16


def shape(*dims):
    return jax.ShapeDtypeStruct(dims, F32)


def to_bf16(x):
    return np.asarray(x, np.float32).astype(BF16)


def split_table(table):
    high = to_bf16(table)
    low = to_bf16(table - high.astype(np.float64))
    return high, low


@functools.lru_cache
def dft_tables(length):
    half = length // 2
    n = np.arange(half)
    forward, backward = [], []
    for odd in (0, 1):
        turn = ((2 * n[:, None] + odd) * n[None, :]) % length
        angle = turn * (2.0 * math.pi / length)
        cos, sin = np.cos(angle) / math.sqrt(length), -np.sin(angle) / math.sqrt(length)
        form = np.block([[cos, -sin], [sin, cos]])
        forward.append(np.stack(split_table(form)))
        backward.append(np.stack(split_table(form.T)))
    place = np.zeros((length, length), np.float32)
    place[2 * n, n] = 1.0
    place[2 * n + 1, half + n] = 1.0
    pick = to_bf16(place)
    return np.stack(forward), np.stack(backward), pick, np.ascontiguousarray(pick.T)


def halves(x):
    high = x.astype(BF16)
    low = (x - high.astype(F32)).astype(BF16)
    return high, low


def left_product(table, x):
    high, low = halves(x)
    return jnp.dot(
        jnp.concatenate([table[0], table[1], table[0]], axis=1),
        jnp.concatenate([high, high, low], axis=0),
        preferred_element_type=F32,
    )


def right_product(x, table):
    high, low = halves(x)
    return jnp.dot(
        jnp.concatenate([high, low, high], axis=1),
        jnp.concatenate([table[0], table[0], table[1]], axis=0),
        preferred_element_type=F32,
    )


def window_masks(offsets, position, win):
    row = offsets[0, 0, position, 0] + HALO
    column = offsets[0, 0, position, 1] + HALO
    low = lax.broadcasted_iota(jnp.int32, (win, win), 0) >= row
    near = lax.broadcasted_iota(jnp.int32, (win, win), 1) >= column
    return low, near


def roll_kernel(offsets, probe, rolled):
    win = probe.shape[1]
    for position in range(rolled.shape[0]):
        row = lax.rem(offsets[0, 0, position, 0] + HALO, win)
        column = lax.rem(offsets[0, 0, position, 1] + HALO, win)
        for plane in (0, 1):
            rolled[position, plane] = pltpu.roll(
                pltpu.roll(probe[plane], column, 1), row, 0
            )


def spread(piece, low, near, upper, lower, win, first):
    above = jnp.where(low, piece, 0.0)
    below = jnp.where(low, 0.0, piece)
    for ref, block in ((upper, above), (lower, below)):
        parts = (jnp.where(near, block, 0.0), jnp.where(near, 0.0, block))
        for lanes, part in zip((slice(0, win), slice(win, None)), parts):
            ref[:, lanes] = part if first else ref[:, lanes] + part


def gradient_kernel(
    place, offsets, near_rows, cross_rows, top, bottom, probe, amplitude, forward, backward,
    grad_near, grad_mid, grad_cross, upper, lower,
):
    count, win, _ = amplitude.shape
    half = win // 2
    is_odd = place[2] > 0

    def patch(plane, low, near):
        up = jnp.where(is_odd, near_rows[plane], cross_rows[plane])
        down = jnp.where(is_odd, cross_rows[plane], near_rows[plane])
        first = jnp.concatenate([up, top[plane]], axis=0)
        second = jnp.concatenate([bottom[plane], down], axis=0)
        return jnp.where(
            near,
            jnp.where(low, first[:, :win], second[:, :win]),
            jnp.where(low, first[:, win:], second[:, win:]),
        )

    for position in range(count):
        low, near = window_masks(offsets, position, win)
        patch_real = patch(0, low, near)
        patch_imag = patch(1, low, near)
        probe_real, probe_imag = probe[position, 0], probe[position, 1]
        real = probe_real * patch_real - probe_imag * patch_imag
        imag = probe_real * patch_imag + probe_imag * patch_real
        summed = jnp.concatenate([real[:half] + real[half:], imag[:half] + imag[half:]], axis=0)
        differ = jnp.concatenate([real[:half] - real[half:], imag[:half] - imag[half:]], axis=0)
        even = left_product(forward[0], summed)
        odd = left_product(forward[1], differ)
        real = jnp.concatenate([even[:half], odd[:half]], axis=0)
        imag = jnp.concatenate([even[half:], odd[half:]], axis=0)
        summed = jnp.concatenate(
            [real[:, :half] + real[:, half:], imag[:, :half] + imag[:, half:]], axis=1
        )
        differ = jnp.concatenate(
            [real[:, :half] - real[:, half:], imag[:, :half] - imag[:, half:]], axis=1
        )
        even = right_product(summed, backward[0])
        odd = right_product(differ, backward[1])
        even_real, even_imag = even[:, :half], even[:, half:]
        odd_real, odd_imag = odd[:, :half], odd[:, half:]
        amp = amplitude[position]
        even_factor = 1.0 - amp[:, :half] * lax.rsqrt(
            even_real * even_real + even_imag * even_imag + smooth_term
        )
        odd_factor = 1.0 - amp[:, half:] * lax.rsqrt(
            odd_real * odd_real + odd_imag * odd_imag + smooth_term
        )
        even = jnp.concatenate([even_factor * even_real, even_factor * even_imag], axis=1)
        odd = jnp.concatenate([odd_factor * odd_real, odd_factor * odd_imag], axis=1)
        even_back = right_product(even, forward[0])
        odd_back = right_product(odd, forward[1])
        summed, differ = even_back + odd_back, even_back - odd_back
        real = jnp.concatenate([summed[:, :half], differ[:, :half]], axis=1)
        imag = jnp.concatenate([summed[:, half:], differ[:, half:]], axis=1)
        even = left_product(backward[0], jnp.concatenate([real[:half], imag[:half]], axis=0))
        odd = left_product(backward[1], jnp.concatenate([real[half:], imag[half:]], axis=0))
        summed, differ = even + odd, even - odd
        real = jnp.concatenate([summed[:half], differ[:half]], axis=0)
        imag = jnp.concatenate([summed[half:], differ[half:]], axis=0)
        for plane, piece in (
            (0, probe_real * real + probe_imag * imag),
            (1, probe_real * imag - probe_imag * real),
        ):
            spread(
                piece, low, near, upper.at[plane], lower.at[plane], win, position == 0
            )
    share(is_odd, upper, lower, grad_near, grad_mid, grad_cross)


def share(is_odd, upper, lower, out_near, out_mid, out_cross):
    edge = out_near.shape[1]
    up, down = upper[:, :edge, :], lower[:, edge:, :]
    out_near[...] = jnp.where(is_odd, up, down)
    out_mid[:, :edge, :] = upper[:, edge:, :]
    out_mid[:, edge:, :] = lower[:, :edge, :]
    out_cross[...] = jnp.where(is_odd, down, up)


def light_kernel(place, offsets, probe, light_near, light_mid, light_cross, upper, lower):
    win = probe.shape[2]
    for position in range(probe.shape[0]):
        low, near = window_masks(offsets, position, win)
        real, imag = probe[position, 0], probe[position, 1]
        spread(
            real * real + imag * imag, low, near, upper.at[0], lower.at[0], win, position == 0
        )
    share(place[2] > 0, upper, lower, light_near, light_mid, light_cross)


def thirds(x):
    high = x.astype(BF16)
    rest = x - high.astype(F32)
    mid = rest.astype(BF16)
    return high, mid, (rest - mid.astype(F32)).astype(BF16)


def order_kernel(amplitude, pick, pick_back, ordered):
    rows = jnp.concatenate([pick_back[...]] * 3, axis=1)
    columns = jnp.concatenate([pick[...]] * 3, axis=0)
    for position in range(ordered.shape[0]):
        block = jnp.dot(
            rows,
            jnp.concatenate(thirds(amplitude[0, 0, position]), axis=0),
            preferred_element_type=F32,
        )
        ordered[position] = jnp.dot(
            jnp.concatenate(thirds(block), axis=1), columns, preferred_element_type=F32
        )


def edges_kernel(specimen, head, tail):
    head[...] = specimen[:, :, :HALO]
    tail[...] = specimen[:, :, specimen.shape[2] - HALO :]


def widen_kernel(place, before, specimen, after, top, bottom, near, cross):
    edge = top.shape[1]
    tile = specimen.shape[2]
    for index, out in enumerate((top, bottom)):
        rows = slice(index * edge, (index + 1) * edge)
        out[:, :, :HALO] = before[:, rows, :]
        out[:, :, HALO : HALO + tile] = specimen[:, rows, :]
        out[:, :, HALO + tile :] = after[:, rows, :]
    sides(place[2] > 0, top, bottom, near, cross)


def sides(is_odd, top, bottom, near, cross):
    near[...] = jnp.where(is_odd, top[...], bottom[...])
    cross[...] = jnp.where(is_odd, bottom[...], top[...])


def fold_rows(place, mid, near, cross):
    is_odd = place[2] > 0
    edge = near.shape[1]
    upper = mid[:, :edge, :] + jnp.where(is_odd, near[...], cross[...])
    lower = mid[:, edge:, :] + jnp.where(is_odd, cross[...], near[...])
    return (slice(0, edge), upper), (slice(edge, None), lower)


def fold_strips_kernel(place, mid, near, cross, head, tail):
    half = head.shape[2]
    for rows, block in fold_rows(place, mid, near, cross):
        head[:, rows, :] = block[:, :, :half]
        tail[:, rows, :] = block[:, :, half:]


def fold_bands_kernel(place, mid, near, cross, head, core, tail):
    tile = core.shape[2]
    for rows, block in fold_rows(place, mid, near, cross):
        head[:, rows, :] = block[:, :, :HALO]
        core[:, rows, :] = block[:, :, HALO : HALO + tile]
        tail[:, rows, :] = block[:, :, HALO + tile :]


def light_sum_kernel(head, tail, from_left, from_right, light, largest):
    left = head[0] + from_left[0]
    right = tail[0] + from_right[0]
    half = left.shape[1]
    light[:, :half] = left
    light[:, half:] = right
    best = jnp.maximum(left[:, HALO:], right[:, : half - HALO])
    rows, columns = best.shape
    found = best[:8]
    for row in range(8, rows, 8):
        found = jnp.maximum(found, best[row : row + 8])
    top = found[:, :LANES]
    for column in range(LANES, columns, LANES):
        top = jnp.maximum(top, found[:, column : column + LANES])
    largest[...] = top


def update_kernel(
    place, head, tail, from_left, from_right, light, peak, old_top, old_bottom,
    top, bottom, near, cross,
):
    edge = top.shape[1]
    half = head.shape[2]
    most = ridge_share * jnp.max(peak[...])
    has_left, has_right = place[0] > 0, place[1] > 0
    lane = lax.broadcasted_iota(jnp.int32, (edge, half), 1)
    keep_left = jnp.logical_or(lane >= HALO, has_left)
    keep_right = jnp.logical_or(lane < half - HALO, has_right)
    for index, (old, out) in enumerate(((old_top, top), (old_bottom, bottom))):
        rows = slice(index * edge, (index + 1) * edge)
        for side, (own, sent, keep) in enumerate(
            ((head, from_left, keep_left), (tail, from_right, keep_right))
        ):
            lanes = slice(side * half, (side + 1) * half)
            scale = 1.0 / (light[rows, lanes] + most)
            for plane in (0, 1):
                gradient = own[plane, rows, :] + sent[plane, rows, :]
                new = old[plane, :, lanes] - gradient * scale
                out[plane, :, lanes] = jnp.where(keep, new, 0.0)
    sides(place[2] > 0, top, bottom, near, cross)


def finish_kernel(core, from_left, from_right, light, peak, old_top, old_bottom, out):
    edge = old_top.shape[1]
    tile = out.shape[2]
    inner = slice(HALO, HALO + tile)
    most = ridge_share * jnp.max(peak[...])
    for index, old in enumerate((old_top, old_bottom)):
        rows = slice(index * edge, (index + 1) * edge)
        scale = 1.0 / (light[rows, inner] + most)
        for plane in (0, 1):
            gradient = core[plane, rows, :]
            gradient = jnp.concatenate(
                [
                    gradient[:, :HALO] + from_left[plane, rows, :],
                    gradient[:, HALO : tile - HALO],
                    gradient[:, tile - HALO :] + from_right[plane, rows, :],
                ],
                axis=1,
            ) if tile > 2 * HALO else jnp.concatenate(
                [
                    gradient[:, :HALO] + from_left[plane, rows, :],
                    gradient[:, HALO:] + from_right[plane, rows, :],
                ],
                axis=1,
            )
            out[plane, rows, :] = old[plane, :, inner] - gradient * scale


def kernel_call(body, outs, specs, flops=0, scratch=(), grant=8):
    moved = 4 * sum(math.prod(out.shape) for out in outs)
    single = len(outs) == 1
    return pl.pallas_call(
        body,
        out_shape=outs[0] if single else outs,
        in_specs=specs,
        out_specs=VM if single else (VM,) * len(outs),
        scratch_shapes=list(scratch),
        compiler_params=pltpu.CompilerParams(vmem_limit_bytes=grant * 1024 * 1024),
        cost_estimate=pl.CostEstimate(
            flops=flops, bytes_accessed=3 * moved, transcendentals=0
        ),
    )


def shifted(block, axis, distance):
    count = lax.axis_size(axis)
    route = [(i - distance, i) for i in range(count) if 0 <= i - distance < count]
    return lax.ppermute(block, axis, route)


def swapped(block, axis, first):
    count = lax.axis_size(axis)
    route = []
    for i in range(first, count - 1, 2):
        route += [(i, i + 1), (i + 1, i)]
    return lax.ppermute(block, axis, route)


def row_exchange(near, cross):
    cross = swapped(cross, "row", 1)
    near = swapped(near, "row", 0)
    return near, cross


def largest_of(block, axes):
    for axis in axes:
        count = lax.axis_size(axis)
        reach = 1
        while reach < count:
            route = [(i, (i + reach) % count) for i in range(count)]
            block = jnp.maximum(block, lax.ppermute(block, axis, route))
            reach *= 2
    return block


def steps(specimen, probe_field, offsets, amplitudes):
    tile = specimen.shape[1]
    win = probe_field.shape[1]
    span = tile + 2 * HALO
    half = span // 2
    count = offsets.shape[2]
    forward, backward, pick, pick_back = [jnp.asarray(t) for t in dft_tables(win)]
    row, col = lax.axis_index("row"), lax.axis_index("col")
    place = jnp.stack([col > 0, col < lax.axis_size("col") - 1, row % 2]).astype(jnp.int32)

    head, tail = kernel_call(edges_kernel, [shape(2, tile, HALO)] * 2, [VM])(specimen)
    before = shifted(tail, "col", 1)
    after = shifted(head, "col", -1)

    probes = kernel_call(roll_kernel, [shape(count, 2, win, win)], [SM, VM])(offsets, probe_field)
    band, middle = shape(1, HALO, span), shape(1, tile, span)
    light_near, light_mid, light_cross = kernel_call(
        light_kernel,
        [band, middle, band],
        [SM, SM, VM],
        scratch=[pltpu.VMEM((1, win, span), F32)] * 2,
    )(place, offsets, probes)
    light_near, light_cross = row_exchange(light_near, light_cross)
    ordered = kernel_call(order_kernel, [shape(count, win, win)], [VM] * 3)(
        amplitudes, pick, pick_back
    )

    block = shape(2, tile // 2, span)
    top, bottom, near, cross = kernel_call(
        widen_kernel, [block] * 4, [SM] + [VM] * 3
    )(place, before, specimen, after)
    near, cross = row_exchange(near, cross)

    light_head, light_tail = kernel_call(
        fold_strips_kernel, [shape(1, tile, half)] * 2, [SM] + [VM] * 3
    )(place, light_mid, light_near, light_cross)
    light_left = shifted(light_tail, "col", 1)
    light_right = shifted(light_head, "col", -1)

    light, peak = None, None
    for iteration in range(ITERS):
        grad_near, grad_mid, grad_cross = kernel_call(
            gradient_kernel,
            [shape(2, HALO, span), shape(2, tile, span), shape(2, HALO, span)],
            [SM] * 2 + [VM] * 8,
            flops=count * 8 * 2 * win * 3 * win * win,
            scratch=[pltpu.VMEM((2, win, span), F32)] * 2,
            grant=24,
        )(
            place, offsets, near, cross, top, bottom, probes, ordered, forward, backward
        )
        grad_near, grad_cross = row_exchange(grad_near, grad_cross)
        if iteration == 0:
            light, found = kernel_call(
                light_sum_kernel, [shape(tile, span), shape(8, LANES)], [VM] * 4
            )(light_head, light_tail, light_left, light_right)
            peak = largest_of(found, ("row", "col"))
        if iteration + 1 < ITERS:
            grad_head, grad_tail = kernel_call(
                fold_strips_kernel, [shape(2, tile, half)] * 2, [SM] + [VM] * 3
            )(place, grad_mid, grad_near, grad_cross)
            from_left = shifted(grad_tail, "col", 1)
            from_right = shifted(grad_head, "col", -1)
            top, bottom, near, cross = kernel_call(
                update_kernel, [block] * 4, [SM] + [VM] * 8
            )(place, grad_head, grad_tail, from_left, from_right, light, peak, top, bottom)
            near, cross = row_exchange(near, cross)
        else:
            head, core, tail = kernel_call(
                fold_bands_kernel,
                [shape(2, tile, HALO), shape(2, tile, tile), shape(2, tile, HALO)],
                [SM] + [VM] * 3,
            )(place, grad_mid, grad_near, grad_cross)
            from_left = shifted(tail, "col", 1)
            from_right = shifted(head, "col", -1)
            return kernel_call(
                finish_kernel, [shape(2, tile, tile)], [VM] * 7
            )(core, from_left, from_right, light, peak, top, bottom)


def solution(mesh):
    return jax.shard_map(
        steps,
        mesh=mesh,
        in_specs=(
            P(None, "row", "col"),
            P(),
            P("row", "col", None, None),
            P("row", "col", None, None, None),
        ),
        out_specs=P(None, "row", "col"),
        check_vma=False,
    )
```

```python
import functools
import math

import jax
import jax.numpy as jnp
import numpy as np
from jax import lax
from jax.experimental import pallas as pl
from jax.experimental.pallas import tpu as pltpu
from jax.sharding import PartitionSpec as P


HALO = 128
ITERS = 2
LANES = 128
ODD, HAS_LEFT, HAS_RIGHT, FLAGS = 0, 1, 2, 3

smooth_term = 0.25
ridge_share = 0.1

VM = pl.BlockSpec(memory_space=pltpu.VMEM)
SM = pl.BlockSpec(memory_space=pltpu.SMEM)
F32 = jnp.float32
BF16 = jnp.bfloat16


def shape(*dims):
    return jax.ShapeDtypeStruct(dims, F32)


def to_bf16(x):
    return np.asarray(x, np.float32).astype(BF16)


def split_table(table):
    high = to_bf16(table)
    low = to_bf16(table - high.astype(np.float64))
    return high, low


@functools.lru_cache
def dft_tables(length):
    half = length // 2
    n = np.arange(half)
    forward, backward = [], []
    for odd in (0, 1):
        turn = ((2 * n[:, None] + odd) * n[None, :]) % length
        angle = turn * (2.0 * math.pi / length)
        cos, sin = np.cos(angle) / math.sqrt(length), -np.sin(angle) / math.sqrt(length)
        form = np.block([[cos, -sin], [sin, cos]])
        forward.append(np.stack(split_table(form)))
        backward.append(np.stack(split_table(form.T)))
    place = np.zeros((length, length), np.float32)
    place[2 * n, n] = 1.0
    place[2 * n + 1, half + n] = 1.0
    pick = to_bf16(place)
    return np.stack(forward), np.stack(backward), pick, np.ascontiguousarray(pick.T)


def halves(x):
    high = x.astype(BF16)
    low = (x - high.astype(F32)).astype(BF16)
    return high, low


def left_product(table, x):
    high, low = halves(x)
    return jnp.dot(
        jnp.concatenate([table[0], table[1], table[0]], axis=1),
        jnp.concatenate([high, high, low], axis=0),
        preferred_element_type=F32,
    )


def right_product(x, table):
    high, low = halves(x)
    return jnp.dot(
        jnp.concatenate([high, low, high], axis=1),
        jnp.concatenate([table[0], table[0], table[1]], axis=0),
        preferred_element_type=F32,
    )


def window_masks(info, position, win):
    at = FLAGS + 2 * position
    low = lax.broadcasted_iota(jnp.int32, (win, win), 0) >= info[at : at + 1, :]
    near = lax.broadcasted_iota(jnp.int32, (win, win), 1) >= info[at + 1 : at + 2, :]
    return low, near


def flag(info, index):
    return info[index : index + 1, :] > 0


def roll_kernel(corners, probe, rolled):
    win = probe.shape[1]
    for position in range(rolled.shape[0]):
        row = lax.rem(corners[2 * position], win)
        column = lax.rem(corners[2 * position + 1], win)
        for plane in (0, 1):
            rolled[position, plane] = pltpu.roll(
                pltpu.roll(probe[plane], column, 1), row, 0
            )


def spread(piece, low, near, quadrants, first):
    above = jnp.where(low, piece, 0.0)
    below = jnp.where(low, 0.0, piece)
    parts = (
        jnp.where(near, above, 0.0), jnp.where(near, 0.0, above),
        jnp.where(near, below, 0.0), jnp.where(near, 0.0, below),
    )
    for index, part in enumerate(parts):
        quadrants[index] = part if first else quadrants[index] + part


def gradient_kernel(
    info, near_inner, cross_inner, near_outer, cross_outer, inner, outer, probe, amplitude,
    forward, backward,
    grad_near_inner, grad_cross_inner, grad_near_outer, grad_cross_outer,
    mid_inner, mid_outer, total,
):
    count, win, _ = amplitude.shape
    half = win // 2
    edge = near_inner.shape[1]
    odd_row = flag(info, ODD)

    def blocks(plane):
        sides = []
        for own, beside, across in (
            (inner, near_inner, cross_inner), (outer, near_outer, cross_outer)
        ):
            up = jnp.where(odd_row, beside[plane], across[plane])
            down = jnp.where(odd_row, across[plane], beside[plane])
            sides.append(
                (
                    jnp.concatenate([up, own[plane, :edge]], axis=0),
                    jnp.concatenate([own[plane, edge:], down], axis=0),
                )
            )
        out = []
        for mid, far in zip(*sides):
            out.append(jnp.concatenate([far[:, :HALO], mid[:, :half]], axis=1))
            out.append(jnp.concatenate([mid[:, half:], far[:, HALO:]], axis=1))
        return out

    def patch(plane, low, near):
        first, second, third, fourth = blocks(plane)
        return jnp.where(
            near, jnp.where(low, first, third), jnp.where(low, second, fourth)
        )

    for position in range(count):
        low, near = window_masks(info, position, win)
        patch_real = patch(0, low, near)
        patch_imag = patch(1, low, near)
        probe_real, probe_imag = probe[position, 0], probe[position, 1]
        real = probe_real * patch_real - probe_imag * patch_imag
        imag = probe_real * patch_imag + probe_imag * patch_real
        summed = jnp.concatenate([real[:half] + real[half:], imag[:half] + imag[half:]], axis=0)
        differ = jnp.concatenate([real[:half] - real[half:], imag[:half] - imag[half:]], axis=0)
        even = left_product(forward[0], summed)
        odd = left_product(forward[1], differ)
        real = jnp.concatenate([even[:half], odd[:half]], axis=0)
        imag = jnp.concatenate([even[half:], odd[half:]], axis=0)
        summed = jnp.concatenate(
            [real[:, :half] + real[:, half:], imag[:, :half] + imag[:, half:]], axis=1
        )
        differ = jnp.concatenate(
            [real[:, :half] - real[:, half:], imag[:, :half] - imag[:, half:]], axis=1
        )
        even = right_product(summed, backward[0])
        odd = right_product(differ, backward[1])
        even_real, even_imag = even[:, :half], even[:, half:]
        odd_real, odd_imag = odd[:, :half], odd[:, half:]
        amp = amplitude[position]
        even_factor = 1.0 - amp[:, :half] * lax.rsqrt(
            even_real * even_real + even_imag * even_imag + smooth_term
        )
        odd_factor = 1.0 - amp[:, half:] * lax.rsqrt(
            odd_real * odd_real + odd_imag * odd_imag + smooth_term
        )
        even = jnp.concatenate([even_factor * even_real, even_factor * even_imag], axis=1)
        odd = jnp.concatenate([odd_factor * odd_real, odd_factor * odd_imag], axis=1)
        even_back = right_product(even, forward[0])
        odd_back = right_product(odd, forward[1])
        summed, differ = even_back + odd_back, even_back - odd_back
        real = jnp.concatenate([summed[:, :half], differ[:, :half]], axis=1)
        imag = jnp.concatenate([summed[:, half:], differ[:, half:]], axis=1)
        even = left_product(backward[0], jnp.concatenate([real[:half], imag[:half]], axis=0))
        odd = left_product(backward[1], jnp.concatenate([real[half:], imag[half:]], axis=0))
        summed, differ = even + odd, even - odd
        real = jnp.concatenate([summed[:half], differ[:half]], axis=0)
        imag = jnp.concatenate([summed[half:], differ[half:]], axis=0)
        for plane, piece in (
            (0, probe_real * real + probe_imag * imag),
            (1, probe_real * imag - probe_imag * real),
        ):
            spread(piece, low, near, total.at[plane], position == 0)
    for plane in (0, 1):
        first, second, third, fourth = [total.at[plane, k] for k in range(4)]
        for take, near_out, cross_out, mid in (
            (
                lambda a, b, rows: jnp.concatenate([a[rows, half:], b[rows, :half]], axis=1),
                grad_near_inner, grad_cross_inner, mid_inner,
            ),
            (
                lambda a, b, rows: jnp.concatenate([a[rows, :HALO], b[rows, win - HALO :]], axis=1),
                grad_near_outer, grad_cross_outer, mid_outer,
            ),
        ):
            up = take(first, second, slice(0, edge))
            down = take(third, fourth, slice(win - edge, win))
            near_out[plane] = jnp.where(odd_row, up, down)
            cross_out[plane] = jnp.where(odd_row, down, up)
            mid[plane, :edge] = take(first, second, slice(edge, win))
            mid[plane, edge:] = take(third, fourth, slice(0, win - edge))


def light_kernel(own_spots, near_spots, cross_spots, odd, probe, light, largest, quadrants):
    win = probe.shape[1]
    half = win // 2
    count = own_spots.shape[0] // 6
    real, imag = probe[0], probe[1]
    intensity = real * real + imag * imag
    quadrants[...] = jnp.zeros_like(quadrants)
    is_odd = odd[0] > 0
    rows = lax.broadcasted_iota(jnp.int32, (half, win), 0)
    columns = lax.broadcasted_iota(jnp.int32, (half, win), 1)

    def spot(row_side, index):
        if row_side == 0:
            return own_spots[index]
        near, cross = near_spots[index], cross_spots[index]
        if row_side < 0:
            return jnp.where(is_odd, near, cross)
        return jnp.where(is_odd, cross, near)

    for row_side in (-1, 0, 1):
        for column_side in (-1, 0, 1):
            base = (column_side + 1) * 2 * count

            @pl.when(spot(row_side, base) > 0)
            def _():
                def one(position, carry):
                    row = spot(row_side, base + 2 * position) - 1
                    column = spot(row_side, base + 2 * position + 1) - 1
                    block = pltpu.roll(intensity, lax.rem(row, win), 0)
                    turn = lax.rem(column, win)
                    for lower in (0, 1):
                        if (row_side < 0 and lower) or (row_side > 0 and not lower):
                            continue
                        part = block[:half] if lower else block[half:]
                        part = pltpu.roll(part, turn, 1)
                        index = rows if lower else rows + half
                        if row_side < 0 or (row_side == 0 and lower):
                            keep = index < row
                        else:
                            keep = index >= row
                        part = jnp.where(keep, part, 0.0)
                        if column_side <= 0:
                            near = columns < column if column_side else columns >= column
                            quadrants[2 * lower] = quadrants[2 * lower] + jnp.where(near, part, 0.0)
                        if column_side >= 0:
                            far = columns >= column if column_side else columns < column
                            quadrants[2 * lower + 1] = quadrants[2 * lower + 1] + jnp.where(far, part, 0.0)
                    return carry

                lax.fori_loop(0, count, one, 0)

    found = None
    for lower in (0, 1):
        out = slice(lower * half, (lower + 1) * half)
        near, far = quadrants[2 * lower], quadrants[2 * lower + 1]
        light[out, :HALO] = near[:, :HALO]
        light[out, HALO : 2 * HALO] = near[:, HALO:]
        light[out, 2 * HALO :] = far
        best = jnp.maximum(near[:, HALO:], far[:, : win - HALO])
        for row in range(0, half, 8):
            block = best[row : row + 8]
            found = block if found is None else jnp.maximum(found, block)
    largest[...] = found


def thirds(x):
    high = x.astype(BF16)
    rest = x - high.astype(F32)
    mid = rest.astype(BF16)
    return high, mid, (rest - mid.astype(F32)).astype(BF16)


def order_kernel(amplitude, pick, pick_back, ordered):
    rows = jnp.concatenate([pick_back[...]] * 3, axis=1)
    columns = jnp.concatenate([pick[...]] * 3, axis=0)
    for position in range(ordered.shape[0]):
        block = jnp.dot(
            rows,
            jnp.concatenate(thirds(amplitude[0, 0, position]), axis=0),
            preferred_element_type=F32,
        )
        ordered[position] = jnp.dot(
            jnp.concatenate(thirds(block), axis=1), columns, preferred_element_type=F32
        )


def edges_kernel(specimen, head, tail):
    head[...] = specimen[:, :, :HALO]
    tail[...] = specimen[:, :, specimen.shape[2] - HALO :]


def row_sides(odd_row, plane, top, bottom, near, cross):
    near[plane] = jnp.where(odd_row, top, bottom)
    cross[plane] = jnp.where(odd_row, bottom, top)


def center_kernel(info, specimen, near, cross):
    edge = near.shape[1]
    odd_row = flag(info, ODD)
    for plane in (0, 1):
        row_sides(odd_row, plane, specimen[plane, :edge], specimen[plane, edge:], near, cross)


def corner_kernel(info, before, after, outer, near, cross):
    edge = near.shape[1]
    odd_row = flag(info, ODD)
    for plane in (0, 1):
        block = jnp.concatenate([before[plane], after[plane]], axis=1)
        outer[plane] = block
        row_sides(odd_row, plane, block[:edge], block[edge:], near, cross)


def folded(odd_row, plane, mid, near, cross):
    edge = near.shape[1]
    upper = mid[plane, :edge] + jnp.where(odd_row, near[plane], cross[plane])
    lower = mid[plane, edge:] + jnp.where(odd_row, cross[plane], near[plane])
    return jnp.concatenate([upper, lower], axis=0)


def fold_kernel(info, mid, near, cross, head, tail):
    odd_row = flag(info, ODD)
    half = head.shape[2]
    for plane in (0, 1):
        block = folded(odd_row, plane, mid, near, cross)
        head[plane] = block[:, :half]
        tail[plane] = block[:, half:]


def inner_light(light):
    return jnp.concatenate([light[:, HALO : 2 * HALO], light[:, 2 * HALO : 3 * HALO]], axis=1)


def outer_light(light):
    return jnp.concatenate([light[:, :HALO], light[:, 3 * HALO :]], axis=1)


def update_inner_kernel(
    info, head, tail, from_left, from_right, light, peak, old, new, near, cross
):
    edge = near.shape[1]
    odd_row = flag(info, ODD)
    scale = 1.0 / (inner_light(light) + ridge_share * jnp.max(peak[...]))
    for plane in (0, 1):
        gradient = jnp.concatenate(
            [head[plane] + from_left[plane], tail[plane] + from_right[plane]], axis=1
        )
        block = old[plane] - gradient * scale
        new[plane] = block
        row_sides(odd_row, plane, block[:edge], block[edge:], near, cross)


def update_outer_kernel(
    info, head, tail, from_left, from_right, light, peak, old, new, near, cross
):
    edge = near.shape[1]
    odd_row = flag(info, ODD)
    lane = lax.broadcasted_iota(jnp.int32, (1, 2 * HALO), 1)
    inside = jnp.where(lane < HALO, info[HAS_LEFT : HAS_LEFT + 1], info[HAS_RIGHT : HAS_RIGHT + 1]) > 0
    scale = 1.0 / (outer_light(light) + ridge_share * jnp.max(peak[...]))
    for plane in (0, 1):
        gradient = jnp.concatenate(
            [head[plane] + from_left[plane], tail[plane] + from_right[plane]], axis=1
        )
        block = jnp.where(inside, old[plane] - gradient * scale, 0.0)
        new[plane] = block
        row_sides(odd_row, plane, block[:edge], block[edge:], near, cross)


def finish_kernel(info, mid, near, cross, from_left, from_right, light, peak, old, out):
    odd_row = flag(info, ODD)
    scale = 1.0 / (inner_light(light) + ridge_share * jnp.max(peak[...]))
    for plane in (0, 1):
        gradient = folded(odd_row, plane, mid, near, cross) + jnp.concatenate(
            [from_left[plane], from_right[plane]], axis=1
        )
        out[plane] = old[plane] - gradient * scale


def kernel_call(body, outs, specs, flops=0, scratch=(), grant=8):
    moved = 4 * sum(math.prod(out.shape) for out in outs)
    single = len(outs) == 1
    return pl.pallas_call(
        body,
        out_shape=outs[0] if single else outs,
        in_specs=specs,
        out_specs=VM if single else (VM,) * len(outs),
        scratch_shapes=list(scratch),
        compiler_params=pltpu.CompilerParams(vmem_limit_bytes=grant * 1024 * 1024),
        cost_estimate=pl.CostEstimate(
            flops=flops, bytes_accessed=3 * moved, transcendentals=0
        ),
    )


def shifted(block, axis, distance):
    count = lax.axis_size(axis)
    route = [(i - distance, i) for i in range(count) if 0 <= i - distance < count]
    return lax.ppermute(block, axis, route)


def swapped(block, axis, first):
    count = lax.axis_size(axis)
    route = []
    for i in range(first, count - 1, 2):
        route += [(i, i + 1), (i + 1, i)]
    return lax.ppermute(block, axis, route)


def row_exchange(near, cross):
    cross = swapped(cross, "row", 1)
    near = swapped(near, "row", 0)
    return near, cross


def largest_of(block, axes):
    for axis in axes:
        count = lax.axis_size(axis)
        reach = 1
        while reach < count:
            route = [(i, (i + reach) % count) for i in range(count)]
            block = jnp.maximum(block, lax.ppermute(block, axis, route))
            reach *= 2
    return block


def steps(specimen, probe_field, offsets, amplitudes):
    tile = specimen.shape[1]
    win = probe_field.shape[1]
    span = tile + 2 * HALO
    count = offsets.shape[2]
    forward, backward, pick, pick_back = [jnp.asarray(t) for t in dft_tables(win)]
    row, col = lax.axis_index("row"), lax.axis_index("col")
    odd = row % 2
    corners = offsets.reshape(-1) + HALO
    flags = jnp.stack([odd, col > 0, col < lax.axis_size("col") - 1]).astype(jnp.int32)
    info = jnp.broadcast_to(
        jnp.concatenate([flags, corners])[:, None], (FLAGS + 2 * count, win)
    )

    spots = corners + 1
    spots_left = shifted(spots, "col", 1)
    spots_right = shifted(spots, "col", -1)

    head, tail = kernel_call(edges_kernel, [shape(2, tile, HALO)] * 2, [VM])(specimen)
    before = shifted(tail, "col", 1)
    after = shifted(head, "col", -1)

    spots = jnp.concatenate([spots_left, spots, spots_right])
    spots_near, spots_cross = row_exchange(spots, spots)

    rows_in = shape(2, tile // 2, tile)
    rows_out = shape(2, tile // 2, 2 * HALO)
    near_in, cross_in = kernel_call(center_kernel, [rows_in] * 2, [VM] * 2)(info, specimen)
    near_in, cross_in = row_exchange(near_in, cross_in)

    probes = kernel_call(roll_kernel, [shape(count, 2, win, win)], [SM, VM])(corners, probe_field)
    ordered = kernel_call(order_kernel, [shape(count, win, win)], [VM] * 3)(
        amplitudes, pick, pick_back
    )
    light, found = kernel_call(
        light_kernel,
        [shape(tile, span), shape(8, LANES)],
        [SM] * 4 + [VM],
        scratch=[pltpu.VMEM((4, win // 2, win), F32)],
    )(spots, spots_near, spots_cross, odd.astype(jnp.int32).reshape(1), probe_field)

    outer, near_out, cross_out = kernel_call(
        corner_kernel, [shape(2, tile, 2 * HALO), rows_out, rows_out], [VM] * 3
    )(info, before, after)
    near_out, cross_out = row_exchange(near_out, cross_out)
    inner = specimen

    peak = largest_of(found, ("col", "row"))
    for step in range(ITERS):
        (
            grad_near_in, grad_cross_in, grad_near_out, grad_cross_out, mid_in, mid_out
        ) = kernel_call(
            gradient_kernel,
            [rows_in] * 2 + [rows_out] * 2 + [shape(2, tile, tile), shape(2, tile, 2 * HALO)],
            [VM] * 11,
            flops=count * 8 * 2 * win * 3 * win * win,
            scratch=[pltpu.VMEM((2, 4, win, win), F32)],
            grant=24,
        )(
            info, near_in, cross_in, near_out, cross_out, inner, outer, probes, ordered,
            forward, backward,
        )
        fold_near, fold_cross = row_exchange(grad_near_out, grad_cross_out)
        head, tail = kernel_call(
            fold_kernel, [shape(2, tile, HALO)] * 2, [VM] * 4
        )(info, mid_out, fold_near, fold_cross)
        to_inner_left = shifted(tail, "col", 1)
        to_inner_right = shifted(head, "col", -1)
        fold_near, fold_cross = row_exchange(grad_near_in, grad_cross_in)
        if step + 1 == ITERS:
            return kernel_call(finish_kernel, [shape(2, tile, tile)], [VM] * 9)(
                info, mid_in, fold_near, fold_cross, to_inner_left, to_inner_right,
                light, peak, inner,
            )
        in_head, in_tail = kernel_call(
            fold_kernel, [shape(2, tile, tile // 2)] * 2, [VM] * 4
        )(info, mid_in, fold_near, fold_cross)
        to_outer_left = shifted(in_tail, "col", 1)
        to_outer_right = shifted(in_head, "col", -1)
        inner, near_in, cross_in = kernel_call(
            update_inner_kernel, [shape(2, tile, tile)] + [rows_in] * 2, [VM] * 8
        )(info, in_head, in_tail, to_inner_left, to_inner_right, light, peak, inner)
        near_in, cross_in = row_exchange(near_in, cross_in)
        outer, near_out, cross_out = kernel_call(
            update_outer_kernel, [shape(2, tile, 2 * HALO)] + [rows_out] * 2, [VM] * 8
        )(info, head, tail, to_outer_left, to_outer_right, light, peak, outer)
        near_out, cross_out = row_exchange(near_out, cross_out)


def solution(mesh):
    return jax.shard_map(
        steps,
        mesh=mesh,
        in_specs=(
            P(None, "row", "col"),
            P(),
            P("row", "col", None, None),
            P("row", "col", None, None, None),
        ),
        out_specs=P(None, "row", "col"),
        check_vma=False,
    )
```

```python
import functools
import math

import jax
import jax.numpy as jnp
import numpy as np
from jax import lax
from jax.experimental import pallas as pl
from jax.experimental.pallas import tpu as pltpu
from jax.sharding import PartitionSpec as P


HALO = 128
ITERS = 2
LANES = 128
ODD, HAS_LEFT, HAS_RIGHT, FLAGS = 0, 1, 2, 3

smooth_term = 0.25
ridge_share = 0.1

VM = pl.BlockSpec(memory_space=pltpu.VMEM)
SM = pl.BlockSpec(memory_space=pltpu.SMEM)
F32 = jnp.float32
BF16 = jnp.bfloat16


def shape(*dims):
    return jax.ShapeDtypeStruct(dims, F32)


def to_bf16(x):
    return np.asarray(x, np.float32).astype(BF16)


def split_table(table):
    high = to_bf16(table)
    low = to_bf16(table - high.astype(np.float64))
    return high, low


@functools.lru_cache
def dft_tables(length):
    half = length // 2
    n = np.arange(half)
    forward, backward = [], []
    for odd in (0, 1):
        turn = ((2 * n[:, None] + odd) * n[None, :]) % length
        angle = turn * (2.0 * math.pi / length)
        cos, sin = np.cos(angle) / math.sqrt(length), -np.sin(angle) / math.sqrt(length)
        form = np.block([[cos, -sin], [sin, cos]])
        forward.append(np.stack(split_table(form)))
        backward.append(np.stack(split_table(form.T)))
    place = np.zeros((length, length), np.float32)
    place[2 * n, n] = 1.0
    place[2 * n + 1, half + n] = 1.0
    pick = to_bf16(place)
    return np.stack(forward), np.stack(backward), pick, np.ascontiguousarray(pick.T)


def halves(x):
    high = x.astype(BF16)
    low = (x - high.astype(F32)).astype(BF16)
    return high, low


def left_product(table, x):
    high, low = halves(x)
    return jnp.dot(
        jnp.concatenate([table[0], table[1], table[0]], axis=1),
        jnp.concatenate([high, high, low], axis=0),
        preferred_element_type=F32,
    )


def right_product(x, table):
    high, low = halves(x)
    return jnp.dot(
        jnp.concatenate([high, low, high], axis=1),
        jnp.concatenate([table[0], table[0], table[1]], axis=0),
        preferred_element_type=F32,
    )


def window_masks(info, position, win):
    at = FLAGS + 2 * position
    low = lax.broadcasted_iota(jnp.int32, (win, win), 0) >= info[at : at + 1, :]
    near = lax.broadcasted_iota(jnp.int32, (win, win), 1) >= info[at + 1 : at + 2, :]
    return low, near


def flag(info, index):
    return info[index : index + 1, :] > 0


def roll_kernel(corners, probe, rolled):
    win = probe.shape[1]
    for position in range(rolled.shape[0]):
        row = lax.rem(corners[2 * position], win)
        column = lax.rem(corners[2 * position + 1], win)
        for plane in (0, 1):
            rolled[position, plane] = pltpu.roll(
                pltpu.roll(probe[plane], column, 1), row, 0
            )


def spread(piece, low, near, quadrants, first):
    above = jnp.where(low, piece, 0.0)
    below = jnp.where(low, 0.0, piece)
    parts = (
        jnp.where(near, above, 0.0), jnp.where(near, 0.0, above),
        jnp.where(near, below, 0.0), jnp.where(near, 0.0, below),
    )
    for index, part in enumerate(parts):
        quadrants[index] = part if first else quadrants[index] + part


def gradient_kernel(
    info, near_rows, cross_rows, near_half, cross_half, probe, amplitude, forward, backward,
    grad_near, grad_cross, mid_near, mid_cross, area, total,
):
    count, win, _ = amplitude.shape
    half = win // 2
    odd_row = flag(info, ODD)
    for plane in (0, 1):
        for left in (0, 1):
            lanes = slice(left * win, (left + 1) * win)
            parts = [ref[plane, :, lanes] for ref in (near_rows, near_half, cross_half, cross_rows)]
            for index in range(4):
                rows = slice((index % 2) * half, (index % 2 + 1) * half)
                area[plane, 2 * (index // 2) + left, rows] = jnp.where(
                    odd_row, parts[index], parts[3 - index]
                )

    def patch(plane, low, near):
        first, second, third, fourth = [area[plane, k] for k in range(4)]
        return jnp.where(
            near, jnp.where(low, first, third), jnp.where(low, second, fourth)
        )

    for position in range(count):
        low, near = window_masks(info, position, win)
        patch_real = patch(0, low, near)
        patch_imag = patch(1, low, near)
        probe_real, probe_imag = probe[position, 0], probe[position, 1]
        real = probe_real * patch_real - probe_imag * patch_imag
        imag = probe_real * patch_imag + probe_imag * patch_real
        summed = jnp.concatenate([real[:half] + real[half:], imag[:half] + imag[half:]], axis=0)
        differ = jnp.concatenate([real[:half] - real[half:], imag[:half] - imag[half:]], axis=0)
        even = left_product(forward[0], summed)
        odd = left_product(forward[1], differ)
        real = jnp.concatenate([even[:half], odd[:half]], axis=0)
        imag = jnp.concatenate([even[half:], odd[half:]], axis=0)
        summed = jnp.concatenate(
            [real[:, :half] + real[:, half:], imag[:, :half] + imag[:, half:]], axis=1
        )
        differ = jnp.concatenate(
            [real[:, :half] - real[:, half:], imag[:, :half] - imag[:, half:]], axis=1
        )
        even = right_product(summed, backward[0])
        odd = right_product(differ, backward[1])
        even_real, even_imag = even[:, :half], even[:, half:]
        odd_real, odd_imag = odd[:, :half], odd[:, half:]
        amp = amplitude[position]
        even_factor = 1.0 - amp[:, :half] * lax.rsqrt(
            even_real * even_real + even_imag * even_imag + smooth_term
        )
        odd_factor = 1.0 - amp[:, half:] * lax.rsqrt(
            odd_real * odd_real + odd_imag * odd_imag + smooth_term
        )
        even = jnp.concatenate([even_factor * even_real, even_factor * even_imag], axis=1)
        odd = jnp.concatenate([odd_factor * odd_real, odd_factor * odd_imag], axis=1)
        even_back = right_product(even, forward[0])
        odd_back = right_product(odd, forward[1])
        summed, differ = even_back + odd_back, even_back - odd_back
        real = jnp.concatenate([summed[:, :half], differ[:, :half]], axis=1)
        imag = jnp.concatenate([summed[:, half:], differ[:, half:]], axis=1)
        even = left_product(backward[0], jnp.concatenate([real[:half], imag[:half]], axis=0))
        odd = left_product(backward[1], jnp.concatenate([real[half:], imag[half:]], axis=0))
        summed, differ = even + odd, even - odd
        real = jnp.concatenate([summed[:half], differ[:half]], axis=0)
        imag = jnp.concatenate([summed[half:], differ[half:]], axis=0)
        for plane, piece in (
            (0, probe_real * real + probe_imag * imag),
            (1, probe_real * imag - probe_imag * real),
        ):
            spread(piece, low, near, total.at[plane], position == 0)
    outs = (grad_near, mid_near, mid_cross, grad_cross)
    for plane in (0, 1):
        for left in (0, 1):
            lanes = slice(left * win, (left + 1) * win)
            parts = [
                total[plane, 2 * (k // 2) + left, (k % 2) * half : (k % 2 + 1) * half]
                for k in range(4)
            ]
            for index in range(4):
                outs[index][plane, :, lanes] = jnp.where(
                    odd_row, parts[index], parts[3 - index]
                )


def light_kernel(
    own_spots, left_spots, right_spots, info, probe, light_near, light_cross, largest, quadrants
):
    win = probe.shape[1]
    half = win // 2
    count = own_spots.shape[0] // 6
    odd_row = flag(info, ODD)
    real, imag = probe[0], probe[1]
    intensity = real * real + imag * imag
    quadrants[...] = jnp.zeros_like(quadrants)
    rows = lax.broadcasted_iota(jnp.int32, (half, win), 0)
    columns = lax.broadcasted_iota(jnp.int32, (half, win), 1)

    for row_side in (-1, 0, 1):
        for column_side, spots in ((-1, left_spots), (0, own_spots), (1, right_spots)):
            base = (row_side + 1) * 2 * count

            @pl.when(spots[base] > 0)
            def _():
                def one(position, carry):
                    row = spots[base + 2 * position] - 1
                    column = spots[base + 2 * position + 1] - 1
                    block = pltpu.roll(intensity, lax.rem(row, win), 0)
                    turn = lax.rem(column, win)
                    for lower in (0, 1):
                        if (row_side < 0 and lower) or (row_side > 0 and not lower):
                            continue
                        part = block[:half] if lower else block[half:]
                        part = pltpu.roll(part, turn, 1)
                        index = rows if lower else rows + half
                        if row_side < 0 or (row_side == 0 and lower):
                            keep = index < row
                        else:
                            keep = index >= row
                        part = jnp.where(keep, part, 0.0)
                        if column_side <= 0:
                            near = columns < column if column_side else columns >= column
                            quadrants[2 * lower] = quadrants[2 * lower] + jnp.where(near, part, 0.0)
                        if column_side >= 0:
                            far = columns >= column if column_side else columns < column
                            quadrants[2 * lower + 1] = quadrants[2 * lower + 1] + jnp.where(far, part, 0.0)
                    return carry

                lax.fori_loop(0, count, one, 0)

    found = None
    for left in (0, 1):
        lanes = slice(left * win, (left + 1) * win)
        upper, lower = quadrants[left], quadrants[2 + left]
        light_near[:, lanes] = jnp.where(odd_row, upper, lower)
        light_cross[:, lanes] = jnp.where(odd_row, lower, upper)
        best = jnp.maximum(upper, lower)
        best = best[:, : win - HALO] if left else best[:, HALO:]
        for row in range(0, half, 8):
            block = best[row : row + 8]
            found = block if found is None else jnp.maximum(found, block)
    largest[...] = found


def thirds(x):
    high = x.astype(BF16)
    rest = x - high.astype(F32)
    mid = rest.astype(BF16)
    return high, mid, (rest - mid.astype(F32)).astype(BF16)


def order_kernel(amplitude, pick, pick_back, ordered):
    rows = jnp.concatenate([pick_back[...]] * 3, axis=1)
    columns = jnp.concatenate([pick[...]] * 3, axis=0)
    for position in range(ordered.shape[0]):
        block = jnp.dot(
            rows,
            jnp.concatenate(thirds(amplitude[0, 0, position]), axis=0),
            preferred_element_type=F32,
        )
        ordered[position] = jnp.dot(
            jnp.concatenate(thirds(block), axis=1), columns, preferred_element_type=F32
        )


def edges_kernel(info, specimen, near_head, near_tail, cross_head, cross_tail):
    odd_row = info[ODD : ODD + 1, :HALO] > 0
    half = near_head.shape[1]
    for plane in (0, 1):
        for lanes, near, cross in (
            (slice(0, HALO), near_head, cross_head),
            (slice(specimen.shape[2] - HALO, None), near_tail, cross_tail),
        ):
            top, bottom = specimen[plane, :half, lanes], specimen[plane, half:, lanes]
            near[plane] = jnp.where(odd_row, top, bottom)
            cross[plane] = jnp.where(odd_row, bottom, top)


def widen_kernel(info, before, specimen, after, out, *, near):
    odd_row = flag(info, ODD)
    half, tile = out.shape[1], specimen.shape[2]
    for plane in (0, 1):
        top, bottom = specimen[plane, :half], specimen[plane, half:]
        own = jnp.where(odd_row, top, bottom) if near else jnp.where(odd_row, bottom, top)
        out[plane, :, :HALO] = before[plane]
        out[plane, :, HALO : HALO + tile] = own
        out[plane, :, HALO + tile :] = after[plane]


def fold_kernel(mid, sent, head, tail):
    side = head.shape[2]
    for plane in (0, 1):
        head[plane] = mid[plane, :, :side] + sent[plane, :, :side]
        tail[plane] = mid[plane, :, side:] + sent[plane, :, side:]


def fold_last_kernel(mid, sent, head, core, tail):
    tile = core.shape[2]
    for plane in (0, 1):
        head[plane] = mid[plane, :, :HALO] + sent[plane, :, :HALO]
        core[plane] = mid[plane, :, HALO : HALO + tile] + sent[plane, :, HALO : HALO + tile]
        tail[plane] = mid[plane, :, HALO + tile :] + sent[plane, :, HALO + tile :]


def update_kernel(info, head, tail, from_left, from_right, light, peak, old, new):
    side = head.shape[2]
    most = ridge_share * jnp.max(peak[...])
    lane = lax.broadcasted_iota(jnp.int32, (1, side), 1)
    for own, sent, inside, lanes in (
        (head, from_left, (lane >= HALO) | flag(info, HAS_LEFT), slice(0, side)),
        (tail, from_right, (lane < side - HALO) | flag(info, HAS_RIGHT), slice(side, None)),
    ):
        scale = 1.0 / (light[:, lanes] + most)
        for plane in (0, 1):
            gradient = own[plane] + sent[plane]
            new[plane, :, lanes] = jnp.where(
                inside, old[plane, :, lanes] - gradient * scale, 0.0
            )


def finish_kernel(info, *refs):
    *halves, peak, out = refs
    odd_row = flag(info, ODD)
    most = ridge_share * jnp.max(peak[...])
    half, tile = out.shape[1] // 2, out.shape[2]
    inner = slice(HALO, HALO + tile)
    for plane in (0, 1):
        news = []
        for core, from_left, from_right, light, old in (halves[:5], halves[5:]):
            sent = [from_left[plane], from_right[plane]]
            if tile > 2 * HALO:
                sent.insert(1, jnp.zeros((half, tile - 2 * HALO), F32))
            gradient = core[plane] + jnp.concatenate(sent, axis=1)
            news.append(old[plane, :, inner] - gradient / (light[:, inner] + most))
        out[plane, :half] = jnp.where(odd_row, news[0], news[1])
        out[plane, half:] = jnp.where(odd_row, news[1], news[0])


def kernel_call(body, outs, specs, flops=0, scratch=(), grant=8):
    moved = 4 * sum(math.prod(out.shape) for out in outs)
    single = len(outs) == 1
    return pl.pallas_call(
        body,
        out_shape=outs[0] if single else outs,
        in_specs=specs,
        out_specs=VM if single else (VM,) * len(outs),
        scratch_shapes=list(scratch),
        compiler_params=pltpu.CompilerParams(vmem_limit_bytes=grant * 1024 * 1024),
        cost_estimate=pl.CostEstimate(
            flops=flops, bytes_accessed=3 * moved, transcendentals=0
        ),
    )


def shifted(block, axis, distance):
    count = lax.axis_size(axis)
    route = [(i - distance, i) for i in range(count) if 0 <= i - distance < count]
    return lax.ppermute(block, axis, route)


def swapped(block, axis, first):
    count = lax.axis_size(axis)
    route = []
    for i in range(first, count - 1, 2):
        route += [(i, i + 1), (i + 1, i)]
    return lax.ppermute(block, axis, route)


def to_cross(block):
    return swapped(block, "row", 1)


def to_near(block):
    return swapped(block, "row", 0)


def to_sides(head, tail):
    right = shifted(tail, "col", 1)
    left = shifted(head, "col", -1)
    return right, left


def largest_of(block, axes):
    for axis in axes:
        count = lax.axis_size(axis)
        reach = 1
        while reach < count:
            route = [(i, (i + reach) % count) for i in range(count)]
            block = jnp.maximum(block, lax.ppermute(block, axis, route))
            reach *= 2
    return block


def steps(specimen, probe_field, offsets, amplitudes):
    tile = specimen.shape[1]
    win = probe_field.shape[1]
    side = tile // 2 + HALO
    half = tile // 2
    count = offsets.shape[2]
    forward, backward, pick, pick_back = [jnp.asarray(t) for t in dft_tables(win)]
    row, col = lax.axis_index("row"), lax.axis_index("col")
    odd = row % 2
    corners = offsets.reshape(-1) + HALO
    flags = jnp.stack([odd, col > 0, col < lax.axis_size("col") - 1]).astype(jnp.int32)
    info = jnp.broadcast_to(
        jnp.concatenate([flags, corners])[:, None], (FLAGS + 2 * count, win)
    )
    band, wide, strip = shape(2, half, HALO), shape(2, half, 2 * side), shape(2, half, side)

    near_head, near_tail, cross_head, cross_tail = kernel_call(
        edges_kernel, [band] * 4, [VM] * 2
    )(info, specimen)
    cross_sides = to_sides(cross_head, cross_tail)
    near_sides = to_sides(near_head, near_tail)

    spots = corners + 1
    spots_cross, spots_near = to_cross(spots), to_near(spots)
    spots = jnp.concatenate(
        [
            jnp.where(odd > 0, spots_near, spots_cross),
            spots,
            jnp.where(odd > 0, spots_cross, spots_near),
        ]
    )
    spots_left, spots_right = to_sides(spots, spots)

    def widened(sides, near):
        return kernel_call(
            functools.partial(widen_kernel, near=near), [wide], [VM] * 4
        )(info, sides[0], specimen, sides[1])

    cross_half = widened(cross_sides, False)
    cross_rows = to_cross(cross_half)
    near_half = widened(near_sides, True)
    near_rows = to_near(near_half)

    probes = kernel_call(roll_kernel, [shape(count, 2, win, win)], [SM, VM])(corners, probe_field)
    ordered = kernel_call(order_kernel, [shape(count, win, win)], [VM] * 3)(
        amplitudes, pick, pick_back
    )
    light_near, light_cross, found = kernel_call(
        light_kernel,
        [shape(half, 2 * side)] * 2 + [shape(8, LANES)],
        [SM] * 3 + [VM] * 2,
        scratch=[pltpu.VMEM((4, half, win), F32)],
    )(spots, spots_left, spots_right, info, probe_field)
    peak = largest_of(found, ("col", "row"))

    for step in range(ITERS):
        grad_near, grad_cross, mid_near, mid_cross = kernel_call(
            gradient_kernel,
            [wide] * 4,
            [VM] * 9,
            flops=count * 8 * 2 * win * 3 * win * win,
            scratch=[pltpu.VMEM((2, 4, win, win), F32)] * 2,
            grant=24,
        )(
            info, near_rows, cross_rows, near_half, cross_half, probes, ordered,
            forward, backward,
        )
        sent_cross = to_cross(grad_cross)
        sent_near = to_near(grad_near)
        if step + 1 < ITERS:
            halves = []
            for mid, sent, light, old in (
                (mid_cross, sent_cross, light_cross, cross_half),
                (mid_near, sent_near, light_near, near_half),
            ):
                head, tail = kernel_call(fold_kernel, [strip] * 2, [VM] * 2)(mid, sent)
                from_left, from_right = to_sides(head, tail)
                halves.append(
                    kernel_call(update_kernel, [wide], [VM] * 8)(
                        info, head, tail, from_left, from_right, light, peak, old
                    )
                )
            cross_half, near_half = halves
            cross_rows = to_cross(cross_half)
            near_rows = to_near(near_half)
        else:
            operands = []
            for mid, sent, light, old in (
                (mid_near, sent_near, light_near, near_half),
                (mid_cross, sent_cross, light_cross, cross_half),
            ):
                head, core, tail = kernel_call(
                    fold_last_kernel, [band, shape(2, half, tile), band], [VM] * 2
                )(mid, sent)
                from_left, from_right = to_sides(head, tail)
                operands += [core, from_left, from_right, light, old]
            return kernel_call(
                finish_kernel, [shape(2, tile, tile)], [VM] * 12
            )(info, *operands, peak)


def solution(mesh):
    return jax.shard_map(
        steps,
        mesh=mesh,
        in_specs=(
            P(None, "row", "col"),
            P(),
            P("row", "col", None, None),
            P("row", "col", None, None, None),
        ),
        out_specs=P(None, "row", "col"),
        check_vma=False,
    )
```

```python
import functools
import math

import jax
import jax.numpy as jnp
import numpy as np
from jax import lax
from jax.experimental import pallas as pl
from jax.experimental.pallas import tpu as pltpu
from jax.sharding import PartitionSpec as P


HALO = 128
ITERS = 2
LANES = 128
ODD, HAS_LEFT, HAS_RIGHT, FLAGS = 0, 1, 2, 3

smooth_term = 0.25
ridge_share = 0.1

VM = pl.BlockSpec(memory_space=pltpu.VMEM)
SM = pl.BlockSpec(memory_space=pltpu.SMEM)
F32 = jnp.float32
BF16 = jnp.bfloat16


def shape(*dims):
    return jax.ShapeDtypeStruct(dims, F32)


def to_bf16(x):
    return np.asarray(x, np.float32).astype(BF16)


def split_table(table):
    high = to_bf16(table)
    low = to_bf16(table - high.astype(np.float64))
    return high, low


@functools.lru_cache
def dft_tables(length):
    half = length // 2
    n = np.arange(half)
    forward, backward = [], []
    for odd in (0, 1):
        turn = ((2 * n[:, None] + odd) * n[None, :]) % length
        angle = turn * (2.0 * math.pi / length)
        cos, sin = np.cos(angle) / math.sqrt(length), -np.sin(angle) / math.sqrt(length)
        form = np.block([[cos, -sin], [sin, cos]])
        forward.append(np.stack(split_table(form)))
        backward.append(np.stack(split_table(form.T)))
    place = np.zeros((length, length), np.float32)
    place[2 * n, n] = 1.0
    place[2 * n + 1, half + n] = 1.0
    pick = to_bf16(place)
    return np.stack(forward), np.stack(backward), pick, np.ascontiguousarray(pick.T)


def halves(x):
    high = x.astype(BF16)
    low = (x - high.astype(F32)).astype(BF16)
    return high, low


def left_product(table, x):
    high, low = halves(x)
    return jnp.dot(
        jnp.concatenate([table[0], table[1], table[0]], axis=1),
        jnp.concatenate([high, high, low], axis=0),
        preferred_element_type=F32,
    )


def right_product(x, table):
    high, low = halves(x)
    return jnp.dot(
        jnp.concatenate([high, low, high], axis=1),
        jnp.concatenate([table[0], table[0], table[1]], axis=0),
        preferred_element_type=F32,
    )


def window_masks(info, position, win):
    at = FLAGS + 2 * position
    low = lax.broadcasted_iota(jnp.int32, (win, win), 0) >= info[at : at + 1, :]
    near = lax.broadcasted_iota(jnp.int32, (win, win), 1) >= info[at + 1 : at + 2, :]
    return low, near


def flag(info, index):
    return info[index : index + 1, :] > 0


def roll_kernel(corners, probe, rolled):
    win = probe.shape[1]
    for position in range(rolled.shape[0]):
        row = lax.rem(corners[2 * position], win)
        column = lax.rem(corners[2 * position + 1], win)
        for plane in (0, 1):
            rolled[position, plane] = pltpu.roll(
                pltpu.roll(probe[plane], column, 1), row, 0
            )


def spread(piece, low, near, quadrants, first):
    above = jnp.where(low, piece, 0.0)
    below = jnp.where(low, 0.0, piece)
    parts = (
        jnp.where(near, above, 0.0), jnp.where(near, 0.0, above),
        jnp.where(near, below, 0.0), jnp.where(near, 0.0, below),
    )
    for index, part in enumerate(parts):
        quadrants[index] = part if first else quadrants[index] + part


def gradient_kernel(
    info, near_rows, cross_rows, near_half, cross_half, probe, amplitude, forward, backward,
    grad_near, grad_cross, mid_near, mid_cross, area, total,
):
    count, win, _ = amplitude.shape
    half = win // 2
    odd_row = flag(info, ODD)
    for plane in (0, 1):
        for left in (0, 1):
            lanes = slice(left * win, (left + 1) * win)
            parts = [ref[plane, :, lanes] for ref in (near_rows, near_half, cross_half, cross_rows)]
            for index in range(4):
                rows = slice((index % 2) * half, (index % 2 + 1) * half)
                area[plane, 2 * (index // 2) + left, rows] = jnp.where(
                    odd_row, parts[index], parts[3 - index]
                )

    def patch(plane, low, near):
        first, second, third, fourth = [area[plane, k] for k in range(4)]
        return jnp.where(
            near, jnp.where(low, first, third), jnp.where(low, second, fourth)
        )

    for position in range(count):
        low, near = window_masks(info, position, win)
        patch_real = patch(0, low, near)
        patch_imag = patch(1, low, near)
        probe_real, probe_imag = probe[position, 0], probe[position, 1]
        real = probe_real * patch_real - probe_imag * patch_imag
        imag = probe_real * patch_imag + probe_imag * patch_real
        summed = jnp.concatenate([real[:half] + real[half:], imag[:half] + imag[half:]], axis=0)
        differ = jnp.concatenate([real[:half] - real[half:], imag[:half] - imag[half:]], axis=0)
        even = left_product(forward[0], summed)
        odd = left_product(forward[1], differ)
        real = jnp.concatenate([even[:half], odd[:half]], axis=0)
        imag = jnp.concatenate([even[half:], odd[half:]], axis=0)
        summed = jnp.concatenate(
            [real[:, :half] + real[:, half:], imag[:, :half] + imag[:, half:]], axis=1
        )
        differ = jnp.concatenate(
            [real[:, :half] - real[:, half:], imag[:, :half] - imag[:, half:]], axis=1
        )
        even = right_product(summed, backward[0])
        odd = right_product(differ, backward[1])
        even_real, even_imag = even[:, :half], even[:, half:]
        odd_real, odd_imag = odd[:, :half], odd[:, half:]
        amp = amplitude[position]
        even_factor = 1.0 - amp[:, :half] * lax.rsqrt(
            even_real * even_real + even_imag * even_imag + smooth_term
        )
        odd_factor = 1.0 - amp[:, half:] * lax.rsqrt(
            odd_real * odd_real + odd_imag * odd_imag + smooth_term
        )
        even = jnp.concatenate([even_factor * even_real, even_factor * even_imag], axis=1)
        odd = jnp.concatenate([odd_factor * odd_real, odd_factor * odd_imag], axis=1)
        even_back = right_product(even, forward[0])
        odd_back = right_product(odd, forward[1])
        summed, differ = even_back + odd_back, even_back - odd_back
        real = jnp.concatenate([summed[:, :half], differ[:, :half]], axis=1)
        imag = jnp.concatenate([summed[:, half:], differ[:, half:]], axis=1)
        even = left_product(backward[0], jnp.concatenate([real[:half], imag[:half]], axis=0))
        odd = left_product(backward[1], jnp.concatenate([real[half:], imag[half:]], axis=0))
        summed, differ = even + odd, even - odd
        real = jnp.concatenate([summed[:half], differ[:half]], axis=0)
        imag = jnp.concatenate([summed[half:], differ[half:]], axis=0)
        for plane, piece in (
            (0, probe_real * real + probe_imag * imag),
            (1, probe_real * imag - probe_imag * real),
        ):
            spread(piece, low, near, total.at[plane], position == 0)
    whole = slice(None)
    for plane in (0, 1):
        by_halves(
            odd_row, total, plane,
            [(out, whole) for out in (grad_near, mid_near, mid_cross, grad_cross)],
        )


def by_halves(odd_row, total, plane, outs):
    half, win = total.shape[2] // 2, total.shape[3]
    for left in (0, 1):
        lanes = slice(left * win, (left + 1) * win)
        parts = [
            total[plane, 2 * (k // 2) + left, (k % 2) * half : (k % 2 + 1) * half]
            for k in range(4)
        ]
        for index, (out, rows) in enumerate(outs):
            out[plane, rows, lanes] = jnp.where(odd_row, parts[index], parts[3 - index])


def light_kernel(info, probe, light_near, light_mid, light_cross, total):
    win = probe.shape[2]
    half = win // 2
    for position in range(probe.shape[0]):
        low, near = window_masks(info, position, win)
        real, imag = probe[position, 0], probe[position, 1]
        spread(real * real + imag * imag, low, near, total.at[0], position == 0)
    whole = slice(None)
    by_halves(
        flag(info, ODD), total, 0,
        (
            (light_near, whole), (light_mid, slice(0, half)),
            (light_mid, slice(half, win)), (light_cross, whole),
        ),
    )


def light_fold_kernel(mid, sent_near, sent_cross, head, tail):
    half, side = sent_near.shape[1], head.shape[2]
    for rows, sent in ((slice(0, half), sent_near), (slice(half, None), sent_cross)):
        block = mid[0, rows] + sent[0]
        head[0, rows] = block[:, :side]
        tail[0, rows] = block[:, side:]


def light_sum_kernel(head, tail, from_left, from_right, light_near, light_cross, largest):
    side = head.shape[2]
    half = light_near.shape[0]
    left, right = head[0] + from_left[0], tail[0] + from_right[0]
    for out, rows in ((light_near, slice(0, half)), (light_cross, slice(half, None))):
        out[:, :side] = left[rows]
        out[:, side:] = right[rows]
    found = None
    for best in (left[:, HALO:], right[:, : side - HALO]):
        for row in range(0, best.shape[0], 8):
            for lane in range(0, best.shape[1], LANES):
                block = best[row : row + 8, lane : lane + LANES]
                found = block if found is None else jnp.maximum(found, block)
    largest[...] = found


def thirds(x):
    high = x.astype(BF16)
    rest = x - high.astype(F32)
    mid = rest.astype(BF16)
    return high, mid, (rest - mid.astype(F32)).astype(BF16)


def order_kernel(amplitude, pick, pick_back, ordered):
    rows = jnp.concatenate([pick_back[...]] * 3, axis=1)
    columns = jnp.concatenate([pick[...]] * 3, axis=0)
    for position in range(ordered.shape[0]):
        block = jnp.dot(
            rows,
            jnp.concatenate(thirds(amplitude[0, 0, position]), axis=0),
            preferred_element_type=F32,
        )
        ordered[position] = jnp.dot(
            jnp.concatenate(thirds(block), axis=1), columns, preferred_element_type=F32
        )


def edges_kernel(specimen, head, tail):
    head[...] = specimen[:, :, :HALO]
    tail[...] = specimen[:, :, specimen.shape[2] - HALO :]


def widen_kernel(info, before, specimen, after, near_half, cross_half):
    odd_row = flag(info, ODD)
    narrow = odd_row[:, :HALO]
    half, tile = near_half.shape[1], specimen.shape[2]
    for plane in (0, 1):
        for source, lanes, odd in (
            (before, slice(0, HALO), narrow),
            (specimen, slice(HALO, HALO + tile), odd_row),
            (after, slice(HALO + tile, None), narrow),
        ):
            top, bottom = source[plane, :half], source[plane, half:]
            near_half[plane, :, lanes] = jnp.where(odd, top, bottom)
            cross_half[plane, :, lanes] = jnp.where(odd, bottom, top)


def fold_kernel(mid, sent, head, tail):
    side = head.shape[2]
    for plane in (0, 1):
        head[plane] = mid[plane, :, :side] + sent[plane, :, :side]
        tail[plane] = mid[plane, :, side:] + sent[plane, :, side:]


def fold_last_kernel(mid, sent, head, core, tail):
    tile = core.shape[2]
    for plane in (0, 1):
        head[plane] = mid[plane, :, :HALO] + sent[plane, :, :HALO]
        core[plane] = mid[plane, :, HALO : HALO + tile] + sent[plane, :, HALO : HALO + tile]
        tail[plane] = mid[plane, :, HALO + tile :] + sent[plane, :, HALO + tile :]


def update_kernel(info, head, tail, from_left, from_right, light, peak, old, new):
    side = head.shape[2]
    most = ridge_share * jnp.max(peak[...])
    lane = lax.broadcasted_iota(jnp.int32, (1, side), 1)
    for own, sent, inside, lanes in (
        (head, from_left, (lane >= HALO) | flag(info, HAS_LEFT), slice(0, side)),
        (tail, from_right, (lane < side - HALO) | flag(info, HAS_RIGHT), slice(side, None)),
    ):
        scale = 1.0 / (light[:, lanes] + most)
        for plane in (0, 1):
            gradient = own[plane] + sent[plane]
            new[plane, :, lanes] = jnp.where(
                inside, old[plane, :, lanes] - gradient * scale, 0.0
            )


def finish_kernel(info, *refs):
    *halves, peak, out = refs
    odd_row = flag(info, ODD)
    most = ridge_share * jnp.max(peak[...])
    half, tile = out.shape[1] // 2, out.shape[2]
    inner = slice(HALO, HALO + tile)
    for plane in (0, 1):
        news = []
        for core, from_left, from_right, light, old in (halves[:5], halves[5:]):
            sent = [from_left[plane], from_right[plane]]
            if tile > 2 * HALO:
                sent.insert(1, jnp.zeros((half, tile - 2 * HALO), F32))
            gradient = core[plane] + jnp.concatenate(sent, axis=1)
            news.append(old[plane, :, inner] - gradient / (light[:, inner] + most))
        out[plane, :half] = jnp.where(odd_row, news[0], news[1])
        out[plane, half:] = jnp.where(odd_row, news[1], news[0])


def kernel_call(body, outs, specs, flops=0, scratch=(), grant=8):
    moved = 4 * sum(math.prod(out.shape) for out in outs)
    single = len(outs) == 1
    return pl.pallas_call(
        body,
        out_shape=outs[0] if single else outs,
        in_specs=specs,
        out_specs=VM if single else (VM,) * len(outs),
        scratch_shapes=list(scratch),
        compiler_params=pltpu.CompilerParams(vmem_limit_bytes=grant * 1024 * 1024),
        cost_estimate=pl.CostEstimate(
            flops=flops, bytes_accessed=3 * moved, transcendentals=0
        ),
    )


def shifted(block, axis, distance):
    count = lax.axis_size(axis)
    route = [(i - distance, i) for i in range(count) if 0 <= i - distance < count]
    return lax.ppermute(block, axis, route)


def swapped(block, axis, first):
    count = lax.axis_size(axis)
    route = []
    for i in range(first, count - 1, 2):
        route += [(i, i + 1), (i + 1, i)]
    return lax.ppermute(block, axis, route)


def to_cross(block):
    return swapped(block, "row", 1)


def to_near(block):
    return swapped(block, "row", 0)


def to_sides(head, tail):
    right = shifted(tail, "col", 1)
    left = shifted(head, "col", -1)
    return right, left


def largest_of(block, axes):
    for axis in axes:
        count = lax.axis_size(axis)
        reach = 1
        while reach < count:
            route = [(i, (i + reach) % count) for i in range(count)]
            block = jnp.maximum(block, lax.ppermute(block, axis, route))
            reach *= 2
    return block


def steps(specimen, probe_field, offsets, amplitudes):
    tile = specimen.shape[1]
    win = probe_field.shape[1]
    side = tile // 2 + HALO
    half = tile // 2
    count = offsets.shape[2]
    forward, backward, pick, pick_back = [jnp.asarray(t) for t in dft_tables(win)]
    row, col = lax.axis_index("row"), lax.axis_index("col")
    odd = row % 2
    corners = offsets.reshape(-1) + HALO
    flags = jnp.stack([odd, col > 0, col < lax.axis_size("col") - 1]).astype(jnp.int32)
    info = jnp.broadcast_to(
        jnp.concatenate([flags, corners])[:, None], (FLAGS + 2 * count, win)
    )
    band, wide, strip = shape(2, half, HALO), shape(2, half, 2 * side), shape(2, half, side)

    head, tail = kernel_call(edges_kernel, [shape(2, tile, HALO)] * 2, [VM])(
        specimen
    )
    before, after = to_sides(head, tail)

    probes = kernel_call(roll_kernel, [shape(count, 2, win, win)], [SM, VM])(corners, probe_field)
    light_band = shape(1, half, 2 * side)
    light_near, light_mid, light_cross = kernel_call(
        light_kernel,
        [light_band, shape(1, tile, 2 * side), light_band],
        [VM] * 2,
        scratch=[pltpu.VMEM((1, 4, win, win), F32)],
    )(info, probes)
    light_cross = to_cross(light_cross)
    light_near = to_near(light_near)
    ordered = kernel_call(order_kernel, [shape(count, win, win)], [VM] * 3)(
        amplitudes, pick, pick_back
    )

    near_half, cross_half = kernel_call(widen_kernel, [wide] * 2, [VM] * 4)(
        info, before, specimen, after
    )
    cross_rows = to_cross(cross_half)
    near_rows = to_near(near_half)

    head, tail = kernel_call(
        light_fold_kernel, [shape(1, tile, side)] * 2, [VM] * 3
    )(light_mid, light_near, light_cross)
    from_left, from_right = to_sides(head, tail)
    light_near, light_cross, found = kernel_call(
        light_sum_kernel, [shape(half, 2 * side)] * 2 + [shape(8, LANES)], [VM] * 4
    )(head, tail, from_left, from_right)
    peak = largest_of(found, ("col", "row"))

    for step in range(ITERS):
        grad_near, grad_cross, mid_near, mid_cross = kernel_call(
            gradient_kernel,
            [wide] * 4,
            [VM] * 9,
            flops=count * 8 * 2 * win * 3 * win * win,
            scratch=[pltpu.VMEM((2, 4, win, win), F32)] * 2,
            grant=24,
        )(
            info, near_rows, cross_rows, near_half, cross_half, probes, ordered,
            forward, backward,
        )
        sent_cross = to_cross(grad_cross)
        sent_near = to_near(grad_near)
        if step + 1 < ITERS:
            halves = []
            for mid, sent, light, old in (
                (mid_cross, sent_cross, light_cross, cross_half),
                (mid_near, sent_near, light_near, near_half),
            ):
                head, tail = kernel_call(fold_kernel, [strip] * 2, [VM] * 2)(mid, sent)
                from_left, from_right = to_sides(head, tail)
                halves.append(
                    kernel_call(update_kernel, [wide], [VM] * 8)(
                        info, head, tail, from_left, from_right, light, peak, old
                    )
                )
            cross_half, near_half = halves
            cross_rows = to_cross(cross_half)
            near_rows = to_near(near_half)
        else:
            operands = []
            for mid, sent, light, old in (
                (mid_near, sent_near, light_near, near_half),
                (mid_cross, sent_cross, light_cross, cross_half),
            ):
                head, core, tail = kernel_call(
                    fold_last_kernel, [band, shape(2, half, tile), band], [VM] * 2
                )(mid, sent)
                from_left, from_right = to_sides(head, tail)
                operands += [core, from_left, from_right, light, old]
            return kernel_call(
                finish_kernel, [shape(2, tile, tile)], [VM] * 12
            )(info, *operands, peak)


def solution(mesh):
    return jax.shard_map(
        steps,
        mesh=mesh,
        in_specs=(
            P(None, "row", "col"),
            P(),
            P("row", "col", None, None),
            P("row", "col", None, None, None),
        ),
        out_specs=P(None, "row", "col"),
        check_vma=False,
    )
```

```python
import functools
import math

import jax
import jax.numpy as jnp
import numpy as np
from jax import lax
from jax.experimental import pallas as pl
from jax.experimental.pallas import tpu as pltpu
from jax.sharding import PartitionSpec as P


HALO = 128
ITERS = 2
LANES = 128
ODD, EVEN_COL, HAS_LEFT, HAS_RIGHT, FLAGS = 0, 1, 2, 3, 4

smooth_term = 0.25
ridge_share = 0.1

VM = pl.BlockSpec(memory_space=pltpu.VMEM)
SM = pl.BlockSpec(memory_space=pltpu.SMEM)
F32 = jnp.float32
BF16 = jnp.bfloat16


def shape(*dims):
    return jax.ShapeDtypeStruct(dims, F32)


def to_bf16(x):
    return np.asarray(x, np.float32).astype(BF16)


def split_table(table):
    high = to_bf16(table)
    low = to_bf16(table - high.astype(np.float64))
    return high, low


@functools.lru_cache
def dft_tables(length):
    half = length // 2
    n = np.arange(half)
    forward, backward = [], []
    for odd in (0, 1):
        turn = ((2 * n[:, None] + odd) * n[None, :]) % length
        angle = turn * (2.0 * math.pi / length)
        cos, sin = np.cos(angle) / math.sqrt(length), -np.sin(angle) / math.sqrt(length)
        form = np.block([[cos, -sin], [sin, cos]])
        forward.append(np.stack(split_table(form)))
        backward.append(np.stack(split_table(form.T)))
    place = np.zeros((length, length), np.float32)
    place[2 * n, n] = 1.0
    place[2 * n + 1, half + n] = 1.0
    pick = to_bf16(place)
    return np.stack(forward), np.stack(backward), pick, np.ascontiguousarray(pick.T)


def halves(x):
    high = x.astype(BF16)
    low = (x - high.astype(F32)).astype(BF16)
    return high, low


def left_product(table, x):
    high, low = halves(x)
    return jnp.dot(
        jnp.concatenate([table[0], table[1], table[0]], axis=1),
        jnp.concatenate([high, high, low], axis=0),
        preferred_element_type=F32,
    )


def right_product(x, table):
    high, low = halves(x)
    return jnp.dot(
        jnp.concatenate([high, low, high], axis=1),
        jnp.concatenate([table[0], table[0], table[1]], axis=0),
        preferred_element_type=F32,
    )


def window_masks(info, position, win):
    at = FLAGS + 2 * position
    low = lax.broadcasted_iota(jnp.int32, (win, win), 0) >= info[at : at + 1, :]
    near = lax.broadcasted_iota(jnp.int32, (win, win), 1) >= info[at + 1 : at + 2, :]
    return low, near


def flag(info, index):
    return info[index : index + 1, :] > 0


def roll_kernel(corners, probe, rolled):
    win = probe.shape[1]
    for position in range(rolled.shape[0]):
        row = lax.rem(corners[2 * position], win)
        column = lax.rem(corners[2 * position + 1], win)
        for plane in (0, 1):
            rolled[position, plane] = pltpu.roll(
                pltpu.roll(probe[plane], column, 1), row, 0
            )


def spread(piece, low, near, quadrants, first):
    above = jnp.where(low, piece, 0.0)
    below = jnp.where(low, 0.0, piece)
    parts = (
        jnp.where(near, above, 0.0), jnp.where(near, 0.0, above),
        jnp.where(near, below, 0.0), jnp.where(near, 0.0, below),
    )
    for index, part in enumerate(parts):
        quadrants[index] = part if first else quadrants[index] + part


def gradient_kernel(
    info, near_rows, cross_rows, near_half, cross_half, probe, amplitude, forward, backward,
    grad_near, grad_cross, mid_near, mid_cross, area, total,
):
    count, win, _ = amplitude.shape
    half = win // 2
    odd_row = flag(info, ODD)
    for plane in (0, 1):
        for left in (0, 1):
            lanes = slice(left * win, (left + 1) * win)
            parts = [ref[plane, :, lanes] for ref in (near_rows, near_half, cross_half, cross_rows)]
            for index in range(4):
                rows = slice((index % 2) * half, (index % 2 + 1) * half)
                area[plane, 2 * (index // 2) + left, rows] = jnp.where(
                    odd_row, parts[index], parts[3 - index]
                )

    def patch(plane, low, near):
        first, second, third, fourth = [area[plane, k] for k in range(4)]
        return jnp.where(
            near, jnp.where(low, first, third), jnp.where(low, second, fourth)
        )

    for position in range(count):
        low, near = window_masks(info, position, win)
        patch_real = patch(0, low, near)
        patch_imag = patch(1, low, near)
        probe_real, probe_imag = probe[position, 0], probe[position, 1]
        real = probe_real * patch_real - probe_imag * patch_imag
        imag = probe_real * patch_imag + probe_imag * patch_real
        summed = jnp.concatenate([real[:half] + real[half:], imag[:half] + imag[half:]], axis=0)
        differ = jnp.concatenate([real[:half] - real[half:], imag[:half] - imag[half:]], axis=0)
        even = left_product(forward[0], summed)
        odd = left_product(forward[1], differ)
        real = jnp.concatenate([even[:half], odd[:half]], axis=0)
        imag = jnp.concatenate([even[half:], odd[half:]], axis=0)
        summed = jnp.concatenate(
            [real[:, :half] + real[:, half:], imag[:, :half] + imag[:, half:]], axis=1
        )
        differ = jnp.concatenate(
            [real[:, :half] - real[:, half:], imag[:, :half] - imag[:, half:]], axis=1
        )
        even = right_product(summed, backward[0])
        odd = right_product(differ, backward[1])
        even_real, even_imag = even[:, :half], even[:, half:]
        odd_real, odd_imag = odd[:, :half], odd[:, half:]
        amp = amplitude[position]
        even_factor = 1.0 - amp[:, :half] * lax.rsqrt(
            even_real * even_real + even_imag * even_imag + smooth_term
        )
        odd_factor = 1.0 - amp[:, half:] * lax.rsqrt(
            odd_real * odd_real + odd_imag * odd_imag + smooth_term
        )
        even = jnp.concatenate([even_factor * even_real, even_factor * even_imag], axis=1)
        odd = jnp.concatenate([odd_factor * odd_real, odd_factor * odd_imag], axis=1)
        even_back = right_product(even, forward[0])
        odd_back = right_product(odd, forward[1])
        summed, differ = even_back + odd_back, even_back - odd_back
        real = jnp.concatenate([summed[:, :half], differ[:, :half]], axis=1)
        imag = jnp.concatenate([summed[:, half:], differ[:, half:]], axis=1)
        even = left_product(backward[0], jnp.concatenate([real[:half], imag[:half]], axis=0))
        odd = left_product(backward[1], jnp.concatenate([real[half:], imag[half:]], axis=0))
        summed, differ = even + odd, even - odd
        real = jnp.concatenate([summed[:half], differ[:half]], axis=0)
        imag = jnp.concatenate([summed[half:], differ[half:]], axis=0)
        for plane, piece in (
            (0, probe_real * real + probe_imag * imag),
            (1, probe_real * imag - probe_imag * real),
        ):
            spread(piece, low, near, total.at[plane], position == 0)
    whole = slice(None)
    for plane in (0, 1):
        by_halves(
            odd_row, total, plane,
            [(out, whole) for out in (grad_near, mid_near, mid_cross, grad_cross)],
        )


def by_halves(odd_row, total, plane, outs):
    half, win = total.shape[2] // 2, total.shape[3]
    for left in (0, 1):
        lanes = slice(left * win, (left + 1) * win)
        parts = [
            total[plane, 2 * (k // 2) + left, (k % 2) * half : (k % 2 + 1) * half]
            for k in range(4)
        ]
        for index, (out, rows) in enumerate(outs):
            out[plane, rows, lanes] = jnp.where(odd_row, parts[index], parts[3 - index])


def light_kernel(info, probe, light_near, light_mid, light_cross, total):
    win = probe.shape[2]
    half = win // 2
    for position in range(probe.shape[0]):
        low, near = window_masks(info, position, win)
        real, imag = probe[position, 0], probe[position, 1]
        spread(real * real + imag * imag, low, near, total.at[0], position == 0)
    whole = slice(None)
    by_halves(
        flag(info, ODD), total, 0,
        (
            (light_near, whole), (light_mid, slice(0, half)),
            (light_mid, slice(half, win)), (light_cross, whole),
        ),
    )


def light_fold_kernel(info, mid, sent_near, sent_cross, close, far):
    even_col = flag(info, EVEN_COL)
    half, side = sent_near.shape[1], close.shape[2]
    for rows, sent in ((slice(0, half), sent_near), (slice(half, None), sent_cross)):
        block = mid[0, rows] + sent[0]
        close[0, rows], far[0, rows] = by_sides(even_col, block[:, :side], block[:, side:])


def light_sum_kernel(
    info, close, far, from_close, from_far, light_near, light_cross, largest
):
    side = close.shape[2]
    half = light_near.shape[0]
    right, left = by_sides(
        flag(info, EVEN_COL), far[0] + from_far[0], close[0] + from_close[0]
    )
    for out, rows in ((light_near, slice(0, half)), (light_cross, slice(half, None))):
        out[:, :side] = left[rows]
        out[:, side:] = right[rows]
    found = None
    for best in (left[:, HALO:], right[:, : side - HALO]):
        for row in range(0, best.shape[0], 8):
            for lane in range(0, best.shape[1], LANES):
                block = best[row : row + 8, lane : lane + LANES]
                found = block if found is None else jnp.maximum(found, block)
    largest[...] = found


def thirds(x):
    high = x.astype(BF16)
    rest = x - high.astype(F32)
    mid = rest.astype(BF16)
    return high, mid, (rest - mid.astype(F32)).astype(BF16)


def order_kernel(amplitude, pick, pick_back, ordered):
    rows = jnp.concatenate([pick_back[...]] * 3, axis=1)
    columns = jnp.concatenate([pick[...]] * 3, axis=0)
    for position in range(ordered.shape[0]):
        block = jnp.dot(
            rows,
            jnp.concatenate(thirds(amplitude[0, 0, position]), axis=0),
            preferred_element_type=F32,
        )
        ordered[position] = jnp.dot(
            jnp.concatenate(thirds(block), axis=1), columns, preferred_element_type=F32
        )


def by_sides(even_col, head, tail):
    even_col = even_col[:, : head.shape[-1]]
    return jnp.where(even_col, tail, head), jnp.where(even_col, head, tail)


def edges_kernel(info, specimen, close, far):
    even_col = flag(info, EVEN_COL)
    for plane in (0, 1):
        close[plane], far[plane] = by_sides(
            even_col, specimen[plane, :, :HALO], specimen[plane, :, specimen.shape[2] - HALO :]
        )


def widen_kernel(info, close, specimen, far, near_half, cross_half):
    odd_row, even_col = flag(info, ODD), flag(info, EVEN_COL)
    half, tile = near_half.shape[1], specimen.shape[2]
    for plane in (0, 1):
        after, before = by_sides(even_col, far[plane], close[plane])
        for source, lanes in (
            (before, slice(0, HALO)),
            (specimen[plane], slice(HALO, HALO + tile)),
            (after, slice(HALO + tile, None)),
        ):
            odd = odd_row[:, : source.shape[1]]
            top, bottom = source[:half], source[half:]
            near_half[plane, :, lanes] = jnp.where(odd, top, bottom)
            cross_half[plane, :, lanes] = jnp.where(odd, bottom, top)


def fold_kernel(info, mid, sent, close, far):
    even_col = flag(info, EVEN_COL)
    side = close.shape[2]
    for plane in (0, 1):
        block = mid[plane] + sent[plane]
        close[plane], far[plane] = by_sides(even_col, block[:, :side], block[:, side:])


def fold_last_kernel(info, mid, sent, close, core, far):
    even_col = flag(info, EVEN_COL)
    tile = core.shape[2]
    for plane in (0, 1):
        block = mid[plane] + sent[plane]
        close[plane], far[plane] = by_sides(even_col, block[:, :HALO], block[:, HALO + tile :])
        core[plane] = block[:, HALO : HALO + tile]


def update_kernel(info, close, far, from_close, from_far, light, peak, old, new):
    even_col = flag(info, EVEN_COL)
    side = close.shape[2]
    most = ridge_share * jnp.max(peak[...])
    lane = lax.broadcasted_iota(jnp.int32, (1, side), 1)
    bounds = (
        ((lane >= HALO) | flag(info, HAS_LEFT), slice(0, side)),
        ((lane < side - HALO) | flag(info, HAS_RIGHT), slice(side, None)),
    )
    scales = [1.0 / (light[:, lanes] + most) for _, lanes in bounds]
    for plane in (0, 1):
        right, left = by_sides(
            even_col, far[plane] + from_far[plane], close[plane] + from_close[plane]
        )
        for gradient, scale, (inside, lanes) in zip((left, right), scales, bounds):
            new[plane, :, lanes] = jnp.where(
                inside, old[plane, :, lanes] - gradient * scale, 0.0
            )


def finish_kernel(info, *refs):
    *halves, peak, out = refs
    odd_row, even_col = flag(info, ODD), flag(info, EVEN_COL)
    most = ridge_share * jnp.max(peak[...])
    half, tile = out.shape[1] // 2, out.shape[2]
    inner = slice(HALO, HALO + tile)
    for plane in (0, 1):
        news = []
        for core, from_close, from_far, light, old in (halves[:5], halves[5:]):
            right, left = by_sides(even_col, from_far[plane], from_close[plane])
            sent = [left, right]
            if tile > 2 * HALO:
                sent.insert(1, jnp.zeros((half, tile - 2 * HALO), F32))
            gradient = core[plane] + jnp.concatenate(sent, axis=1)
            news.append(old[plane, :, inner] - gradient / (light[:, inner] + most))
        out[plane, :half] = jnp.where(odd_row, news[0], news[1])
        out[plane, half:] = jnp.where(odd_row, news[1], news[0])


def kernel_call(body, outs, specs, flops=0, scratch=(), grant=8):
    moved = 4 * sum(math.prod(out.shape) for out in outs)
    single = len(outs) == 1
    return pl.pallas_call(
        body,
        out_shape=outs[0] if single else outs,
        in_specs=specs,
        out_specs=VM if single else (VM,) * len(outs),
        scratch_shapes=list(scratch),
        compiler_params=pltpu.CompilerParams(vmem_limit_bytes=grant * 1024 * 1024),
        cost_estimate=pl.CostEstimate(
            flops=flops, bytes_accessed=3 * moved, transcendentals=0
        ),
    )


def swapped(block, axis, first):
    count = lax.axis_size(axis)
    route = []
    for i in range(first, count - 1, 2):
        route += [(i, i + 1), (i + 1, i)]
    return lax.ppermute(block, axis, route)


def to_cross(block):
    return swapped(block, "row", 1)


def to_near(block):
    return swapped(block, "row", 0)


def to_sides(close, far):
    close = swapped(close, "col", 0)
    far = swapped(far, "col", 1)
    return close, far


def largest_of(block, axes):
    for axis in axes:
        count = lax.axis_size(axis)
        reach = 1
        while reach < count:
            if count & (count - 1) == 0:
                route = [(i, i ^ reach) for i in range(count)]
            else:
                route = [(i, (i + reach) % count) for i in range(count)]
            block = jnp.maximum(block, lax.ppermute(block, axis, route))
            reach *= 2
    return block


def steps(specimen, probe_field, offsets, amplitudes):
    tile = specimen.shape[1]
    win = probe_field.shape[1]
    side = tile // 2 + HALO
    half = tile // 2
    count = offsets.shape[2]
    forward, backward, pick, pick_back = [jnp.asarray(t) for t in dft_tables(win)]
    row, col = lax.axis_index("row"), lax.axis_index("col")
    odd = row % 2
    corners = offsets.reshape(-1) + HALO
    flags = jnp.stack([odd, (col + 1) % 2, col > 0, col < lax.axis_size("col") - 1]).astype(jnp.int32)
    info = jnp.broadcast_to(
        jnp.concatenate([flags, corners])[:, None], (FLAGS + 2 * count, win)
    )
    band, wide, strip = shape(2, half, HALO), shape(2, half, 2 * side), shape(2, half, side)

    close, far = kernel_call(edges_kernel, [shape(2, tile, HALO)] * 2, [VM] * 2)(info, specimen)
    close, far = to_sides(close, far)

    probes = kernel_call(roll_kernel, [shape(count, 2, win, win)], [SM, VM])(corners, probe_field)
    light_band = shape(1, half, 2 * side)
    light_near, light_mid, light_cross = kernel_call(
        light_kernel,
        [light_band, shape(1, tile, 2 * side), light_band],
        [VM] * 2,
        scratch=[pltpu.VMEM((1, 4, win, win), F32)],
    )(info, probes)
    light_cross = to_cross(light_cross)
    light_near = to_near(light_near)
    ordered = kernel_call(order_kernel, [shape(count, win, win)], [VM] * 3)(
        amplitudes, pick, pick_back
    )

    near_half, cross_half = kernel_call(widen_kernel, [wide] * 2, [VM] * 4)(
        info, close, specimen, far
    )
    cross_rows = to_cross(cross_half)
    near_rows = to_near(near_half)

    close, far = kernel_call(
        light_fold_kernel, [shape(1, tile, side)] * 2, [VM] * 4
    )(info, light_mid, light_near, light_cross)
    from_close, from_far = to_sides(close, far)
    light_near, light_cross, found = kernel_call(
        light_sum_kernel, [shape(half, 2 * side)] * 2 + [shape(8, LANES)], [VM] * 5
    )(info, close, far, from_close, from_far)
    peak = largest_of(found, ("col", "row"))

    for step in range(ITERS):
        grad_near, grad_cross, mid_near, mid_cross = kernel_call(
            gradient_kernel,
            [wide] * 4,
            [VM] * 9,
            flops=count * 8 * 2 * win * 3 * win * win,
            scratch=[pltpu.VMEM((2, 4, win, win), F32)] * 2,
            grant=24,
        )(
            info, near_rows, cross_rows, near_half, cross_half, probes, ordered,
            forward, backward,
        )
        sent_cross = to_cross(grad_cross)
        sent_near = to_near(grad_near)
        if step + 1 < ITERS:
            halves = []
            for mid, sent, light, old in (
                (mid_cross, sent_cross, light_cross, cross_half),
                (mid_near, sent_near, light_near, near_half),
            ):
                close, far = kernel_call(fold_kernel, [strip] * 2, [VM] * 3)(info, mid, sent)
                from_close, from_far = to_sides(close, far)
                halves.append(
                    kernel_call(update_kernel, [wide], [VM] * 8)(
                        info, close, far, from_close, from_far, light, peak, old
                    )
                )
            cross_half, near_half = halves
            cross_rows = to_cross(cross_half)
            near_rows = to_near(near_half)
        else:
            operands = []
            for mid, sent, light, old in (
                (mid_near, sent_near, light_near, near_half),
                (mid_cross, sent_cross, light_cross, cross_half),
            ):
                close, core, far = kernel_call(
                    fold_last_kernel, [band, shape(2, half, tile), band], [VM] * 3
                )(info, mid, sent)
                from_close, from_far = to_sides(close, far)
                operands += [core, from_close, from_far, light, old]
            return kernel_call(
                finish_kernel, [shape(2, tile, tile)], [VM] * 12
            )(info, *operands, peak)


def solution(mesh):
    return jax.shard_map(
        steps,
        mesh=mesh,
        in_specs=(
            P(None, "row", "col"),
            P(),
            P("row", "col", None, None),
            P("row", "col", None, None, None),
        ),
        out_specs=P(None, "row", "col"),
        check_vma=False,
    )
```

```python
import functools
import math

import jax
import jax.numpy as jnp
import numpy as np
from jax import lax
from jax.experimental import pallas as pl
from jax.experimental.pallas import tpu as pltpu
from jax.sharding import PartitionSpec as P


HALO = 128
ITERS = 2
LANES = 128
ODD, EVEN_COL, HAS_LEFT, HAS_RIGHT, FLAGS = 0, 1, 2, 3, 4

smooth_term = 0.25
ridge_share = 0.1

VM = pl.BlockSpec(memory_space=pltpu.VMEM)
SM = pl.BlockSpec(memory_space=pltpu.SMEM)
F32 = jnp.float32
BF16 = jnp.bfloat16


def shape(*dims):
    return jax.ShapeDtypeStruct(dims, F32)


def to_bf16(x):
    return np.asarray(x, np.float32).astype(BF16)


def split_table(table):
    high = to_bf16(table)
    low = to_bf16(table - high.astype(np.float64))
    return high, low


@functools.lru_cache
def dft_tables(length):
    half = length // 2
    n = np.arange(half)
    forward, backward = [], []
    for odd in (0, 1):
        turn = ((2 * n[:, None] + odd) * n[None, :]) % length
        angle = turn * (2.0 * math.pi / length)
        cos, sin = np.cos(angle) / math.sqrt(length), -np.sin(angle) / math.sqrt(length)
        form = np.block([[cos, -sin], [sin, cos]])
        forward.append(np.stack(split_table(form)))
        backward.append(np.stack(split_table(form.T)))
    place = np.zeros((length, length), np.float32)
    place[2 * n, n] = 1.0
    place[2 * n + 1, half + n] = 1.0
    pick = to_bf16(place)
    return np.stack(forward), np.stack(backward), pick, np.ascontiguousarray(pick.T)


def halves(x):
    high = x.astype(BF16)
    low = (x - high.astype(F32)).astype(BF16)
    return high, low


def left_product(table, x):
    high, low = halves(x)
    return jnp.dot(
        jnp.concatenate([table[0], table[1], table[0]], axis=1),
        jnp.concatenate([high, high, low], axis=0),
        preferred_element_type=F32,
    )


def right_product(x, table):
    high, low = halves(x)
    return jnp.dot(
        jnp.concatenate([high, low, high], axis=1),
        jnp.concatenate([table[0], table[0], table[1]], axis=0),
        preferred_element_type=F32,
    )


def window_masks(info, position, win):
    at = FLAGS + 2 * position
    low = lax.broadcasted_iota(jnp.int32, (win, win), 0) >= info[at : at + 1, :]
    near = lax.broadcasted_iota(jnp.int32, (win, win), 1) >= info[at + 1 : at + 2, :]
    return low, near


def flag(info, index):
    return info[index : index + 1, :] > 0


def roll_kernel(corners, probe, rolled):
    win = probe.shape[1]
    for position in range(rolled.shape[0]):
        row = lax.rem(corners[2 * position], win)
        column = lax.rem(corners[2 * position + 1], win)
        for plane in (0, 1):
            rolled[position, plane] = pltpu.roll(
                pltpu.roll(probe[plane], column, 1), row, 0
            )


def spread(piece, low, near, quadrants, first):
    above = jnp.where(low, piece, 0.0)
    below = jnp.where(low, 0.0, piece)
    parts = (
        jnp.where(near, above, 0.0), jnp.where(near, 0.0, above),
        jnp.where(near, below, 0.0), jnp.where(near, 0.0, below),
    )
    for index, part in enumerate(parts):
        quadrants[index] = part if first else quadrants[index] + part


def load_side(ref, plane, left, win):
    if not isinstance(ref, tuple):
        return ref[plane, :, left * win : (left + 1) * win]
    inner, outer = ref
    half = win - HALO
    if left:
        return jnp.concatenate([inner[plane, :, half:], outer[plane, :, HALO:]], axis=1)
    return jnp.concatenate([outer[plane, :, :HALO], inner[plane, :, :half]], axis=1)


def store_side(ref, plane, rows, left, value):
    win = value.shape[1]
    if not isinstance(ref, tuple):
        ref[plane, rows, left * win : (left + 1) * win] = value
        return
    inner, outer = ref
    half = win - HALO
    if left:
        inner[plane, rows, half:] = value[:, :half]
        outer[plane, rows, HALO:] = value[:, half:]
    else:
        outer[plane, rows, :HALO] = value[:, :HALO]
        inner[plane, rows, :half] = value[:, HALO:]


def gradient_kernel(*refs, first, last):
    refs = list(refs)
    if first:
        refs[2:4] = [tuple(refs[2:4])]
    if last:
        refs[10:12] = [tuple(refs[10:12])]
    gradient_body(*refs)


def gradient_body(
    info, near_rows, cross_rows, near_half, cross_half, probe, amplitude, forward, backward,
    grad_near, grad_cross, mid_near, mid_cross, area, total,
):
    count, win, _ = amplitude.shape
    half = win // 2
    odd_row = flag(info, ODD)
    for plane in (0, 1):
        for left in (0, 1):
            parts = [
                load_side(ref, plane, left, win)
                for ref in (near_rows, near_half, cross_half, cross_rows)
            ]
            for index in range(4):
                rows = slice((index % 2) * half, (index % 2 + 1) * half)
                area[plane, 2 * (index // 2) + left, rows] = jnp.where(
                    odd_row, parts[index], parts[3 - index]
                )

    def patch(plane, low, near):
        first, second, third, fourth = [area[plane, k] for k in range(4)]
        return jnp.where(
            near, jnp.where(low, first, third), jnp.where(low, second, fourth)
        )

    for position in range(count):
        low, near = window_masks(info, position, win)
        patch_real = patch(0, low, near)
        patch_imag = patch(1, low, near)
        probe_real, probe_imag = probe[position, 0], probe[position, 1]
        real = probe_real * patch_real - probe_imag * patch_imag
        imag = probe_real * patch_imag + probe_imag * patch_real
        summed = jnp.concatenate([real[:half] + real[half:], imag[:half] + imag[half:]], axis=0)
        differ = jnp.concatenate([real[:half] - real[half:], imag[:half] - imag[half:]], axis=0)
        even = left_product(forward[0], summed)
        odd = left_product(forward[1], differ)
        real = jnp.concatenate([even[:half], odd[:half]], axis=0)
        imag = jnp.concatenate([even[half:], odd[half:]], axis=0)
        summed = jnp.concatenate(
            [real[:, :half] + real[:, half:], imag[:, :half] + imag[:, half:]], axis=1
        )
        differ = jnp.concatenate(
            [real[:, :half] - real[:, half:], imag[:, :half] - imag[:, half:]], axis=1
        )
        even = right_product(summed, backward[0])
        odd = right_product(differ, backward[1])
        even_real, even_imag = even[:, :half], even[:, half:]
        odd_real, odd_imag = odd[:, :half], odd[:, half:]
        amp = amplitude[position]
        even_factor = 1.0 - amp[:, :half] * lax.rsqrt(
            even_real * even_real + even_imag * even_imag + smooth_term
        )
        odd_factor = 1.0 - amp[:, half:] * lax.rsqrt(
            odd_real * odd_real + odd_imag * odd_imag + smooth_term
        )
        even = jnp.concatenate([even_factor * even_real, even_factor * even_imag], axis=1)
        odd = jnp.concatenate([odd_factor * odd_real, odd_factor * odd_imag], axis=1)
        even_back = right_product(even, forward[0])
        odd_back = right_product(odd, forward[1])
        summed, differ = even_back + odd_back, even_back - odd_back
        real = jnp.concatenate([summed[:, :half], differ[:, :half]], axis=1)
        imag = jnp.concatenate([summed[:, half:], differ[:, half:]], axis=1)
        even = left_product(backward[0], jnp.concatenate([real[:half], imag[:half]], axis=0))
        odd = left_product(backward[1], jnp.concatenate([real[half:], imag[half:]], axis=0))
        summed, differ = even + odd, even - odd
        real = jnp.concatenate([summed[:half], differ[:half]], axis=0)
        imag = jnp.concatenate([summed[half:], differ[half:]], axis=0)
        for plane, piece in (
            (0, probe_real * real + probe_imag * imag),
            (1, probe_real * imag - probe_imag * real),
        ):
            spread(piece, low, near, total.at[plane], position == 0)
    whole = slice(None)
    for plane in (0, 1):
        by_halves(
            odd_row, total, plane,
            [(out, whole) for out in (grad_near, mid_near, mid_cross, grad_cross)],
        )


def by_halves(odd_row, total, plane, outs):
    half = total.shape[2] // 2
    for left in (0, 1):
        parts = [
            total[plane, 2 * (k // 2) + left, (k % 2) * half : (k % 2 + 1) * half]
            for k in range(4)
        ]
        for index, (out, rows) in enumerate(outs):
            store_side(
                out, plane, rows, left, jnp.where(odd_row, parts[index], parts[3 - index])
            )


def light_kernel(info, probe, light_near, light_mid, light_cross, total):
    win = probe.shape[2]
    half = win // 2
    for position in range(probe.shape[0]):
        low, near = window_masks(info, position, win)
        real, imag = probe[position, 0], probe[position, 1]
        spread(real * real + imag * imag, low, near, total.at[0], position == 0)
    whole = slice(None)
    by_halves(
        flag(info, ODD), total, 0,
        (
            (light_near, whole), (light_mid, slice(0, half)),
            (light_mid, slice(half, win)), (light_cross, whole),
        ),
    )


def light_fold_kernel(info, mid, sent_near, sent_cross, close, far):
    even_col = flag(info, EVEN_COL)
    half, side = sent_near.shape[1], close.shape[2]
    for rows, sent in ((slice(0, half), sent_near), (slice(half, None), sent_cross)):
        block = mid[0, rows] + sent[0]
        close[0, rows], far[0, rows] = by_sides(even_col, block[:, :side], block[:, side:])


def light_sum_kernel(
    info, close, far, from_close, from_far, light_near, light_cross, largest
):
    side = close.shape[2]
    half = light_near.shape[0]
    right, left = by_sides(
        flag(info, EVEN_COL), far[0] + from_far[0], close[0] + from_close[0]
    )
    for out, rows in ((light_near, slice(0, half)), (light_cross, slice(half, None))):
        out[:, :side] = left[rows]
        out[:, side:] = right[rows]
    found = None
    for best in (left[:, HALO:], right[:, : side - HALO]):
        for row in range(0, best.shape[0], 8):
            for lane in range(0, best.shape[1], LANES):
                block = best[row : row + 8, lane : lane + LANES]
                found = block if found is None else jnp.maximum(found, block)
    largest[...] = found


def thirds(x):
    high = x.astype(BF16)
    rest = x - high.astype(F32)
    mid = rest.astype(BF16)
    return high, mid, (rest - mid.astype(F32)).astype(BF16)


def order_kernel(amplitude, pick, pick_back, ordered):
    rows = jnp.concatenate([pick_back[...]] * 3, axis=1)
    columns = jnp.concatenate([pick[...]] * 3, axis=0)
    for position in range(ordered.shape[0]):
        block = jnp.dot(
            rows,
            jnp.concatenate(thirds(amplitude[0, 0, position]), axis=0),
            preferred_element_type=F32,
        )
        ordered[position] = jnp.dot(
            jnp.concatenate(thirds(block), axis=1), columns, preferred_element_type=F32
        )


def by_sides(even_col, head, tail):
    even_col = even_col[:, : head.shape[-1]]
    return jnp.where(even_col, tail, head), jnp.where(even_col, head, tail)


def edges_kernel(specimen, close, far):
    even_col = lax.axis_index("col") % 2 == 0
    for plane in (0, 1):
        head, tail = specimen[plane, :, :HALO], specimen[plane, :, specimen.shape[2] - HALO :]
        close[plane] = jnp.where(even_col, tail, head)
        far[plane] = jnp.where(even_col, head, tail)


def center_kernel(info, specimen, cross):
    odd_row = flag(info, ODD)
    half = cross.shape[1]
    for plane in (0, 1):
        cross[plane] = jnp.where(odd_row, specimen[plane, half:], specimen[plane, :half])


def widen_kernel(info, close, specimen, far, near_half, cross_half, cross_outer):
    odd_row, even_col = flag(info, ODD), flag(info, EVEN_COL)
    half, tile = near_half.shape[1], specimen.shape[2]
    for plane in (0, 1):
        after, before = by_sides(even_col, far[plane], close[plane])
        for source, lanes in (
            (before, slice(0, HALO)),
            (specimen[plane], slice(HALO, HALO + tile)),
            (after, slice(HALO + tile, None)),
        ):
            odd = odd_row[:, : source.shape[1]]
            top, bottom = source[:half], source[half:]
            near_half[plane, :, lanes] = jnp.where(odd, top, bottom)
            cross_half[plane, :, lanes] = jnp.where(odd, bottom, top)
        cross_outer[plane, :, :HALO] = cross_half[plane, :, :HALO]
        cross_outer[plane, :, HALO:] = cross_half[plane, :, HALO + tile :]


def fold_kernel(info, mid, sent, close, far):
    even_col = flag(info, EVEN_COL)
    side = close.shape[2]
    for plane in (0, 1):
        block = mid[plane] + sent[plane]
        close[plane], far[plane] = by_sides(even_col, block[:, :side], block[:, side:])


def fold_last_kernel(info, mid, sent, close, far):
    even_col = flag(info, EVEN_COL)
    for plane in (0, 1):
        head = mid[plane, :, :HALO] + sent[plane, :, :HALO]
        tail = mid[plane, :, mid.shape[2] - HALO :] + sent[plane, :, sent.shape[2] - HALO :]
        close[plane], far[plane] = by_sides(even_col, head, tail)


def update_kernel(info, close, far, from_close, from_far, light, peak, old, new):
    even_col = flag(info, EVEN_COL)
    side = close.shape[2]
    most = ridge_share * jnp.max(peak[...])
    lane = lax.broadcasted_iota(jnp.int32, (1, side), 1)
    bounds = (
        ((lane >= HALO) | flag(info, HAS_LEFT), slice(0, side)),
        ((lane < side - HALO) | flag(info, HAS_RIGHT), slice(side, None)),
    )
    scales = [1.0 / (light[:, lanes] + most) for _, lanes in bounds]
    for plane in (0, 1):
        right, left = by_sides(
            even_col, far[plane] + from_far[plane], close[plane] + from_close[plane]
        )
        for gradient, scale, (inside, lanes) in zip((left, right), scales, bounds):
            new[plane, :, lanes] = jnp.where(
                inside, old[plane, :, lanes] - gradient * scale, 0.0
            )


def finish_kernel(info, *refs):
    *halves, peak, out = refs
    odd_row, even_col = flag(info, ODD), flag(info, EVEN_COL)
    most = ridge_share * jnp.max(peak[...])
    half, tile = out.shape[1] // 2, out.shape[2]
    inner = slice(HALO, HALO + tile)
    for plane in (0, 1):
        news = []
        for mid, add, from_close, from_far, light, old in (halves[:6], halves[6:]):
            right, left = by_sides(even_col, from_far[plane], from_close[plane])
            sent = [left, right]
            if tile > 2 * HALO:
                sent.insert(1, jnp.zeros((half, tile - 2 * HALO), F32))
            add = add[plane] if add.shape[2] == tile else add[plane, :, inner]
            gradient = mid[plane, :, inner] + add + jnp.concatenate(sent, axis=1)
            news.append(old[plane, :, inner] - gradient / (light[:, inner] + most))
        out[plane, :half] = jnp.where(odd_row, news[0], news[1])
        out[plane, half:] = jnp.where(odd_row, news[1], news[0])


def kernel_call(body, outs, specs, flops=0, scratch=(), grant=8):
    moved = 4 * sum(math.prod(out.shape) for out in outs)
    single = len(outs) == 1
    return pl.pallas_call(
        body,
        out_shape=outs[0] if single else outs,
        in_specs=specs,
        out_specs=VM if single else (VM,) * len(outs),
        scratch_shapes=list(scratch),
        compiler_params=pltpu.CompilerParams(vmem_limit_bytes=grant * 1024 * 1024),
        cost_estimate=pl.CostEstimate(
            flops=flops, bytes_accessed=3 * moved, transcendentals=0
        ),
    )


def swapped(block, axis, first):
    count = lax.axis_size(axis)
    route = []
    for i in range(first, count - 1, 2):
        route += [(i, i + 1), (i + 1, i)]
    return lax.ppermute(block, axis, route)


def to_cross(block):
    return swapped(block, "row", 1)


def to_near(block):
    return swapped(block, "row", 0)


def to_sides(close, far):
    close = swapped(close, "col", 0)
    far = swapped(far, "col", 1)
    return close, far


def largest_of(block, axes):
    for axis in axes:
        count = lax.axis_size(axis)
        reach = 1
        while reach < count:
            if count & (count - 1) == 0:
                route = [(i, i ^ reach) for i in range(count)]
            else:
                route = [(i, (i + reach) % count) for i in range(count)]
            block = jnp.maximum(block, lax.ppermute(block, axis, route))
            reach *= 2
    return block


def steps(specimen, probe_field, offsets, amplitudes):
    tile = specimen.shape[1]
    win = probe_field.shape[1]
    side = tile // 2 + HALO
    half = tile // 2
    count = offsets.shape[2]
    forward, backward, pick, pick_back = [jnp.asarray(t) for t in dft_tables(win)]
    row, col = lax.axis_index("row"), lax.axis_index("col")
    odd = row % 2
    corners = offsets.reshape(-1) + HALO
    flags = jnp.stack([odd, (col + 1) % 2, col > 0, col < lax.axis_size("col") - 1]).astype(jnp.int32)
    info = jnp.broadcast_to(
        jnp.concatenate([flags, corners])[:, None], (FLAGS + 2 * count, win)
    )
    band, wide, strip = shape(2, half, HALO), shape(2, half, 2 * side), shape(2, half, side)
    inner, outer = shape(2, half, tile), shape(2, half, 2 * HALO)

    close, far = kernel_call(edges_kernel, [shape(2, tile, HALO)] * 2, [VM])(
        specimen
    )
    close, far = to_sides(close, far)

    cross_inner = to_cross(kernel_call(center_kernel, [inner], [VM] * 2)(info, specimen))

    probes = kernel_call(roll_kernel, [shape(count, 2, win, win)], [SM, VM])(corners, probe_field)
    light_band = shape(1, half, 2 * side)
    light_near, light_mid, light_cross = kernel_call(
        light_kernel,
        [light_band, shape(1, tile, 2 * side), light_band],
        [VM] * 2,
        scratch=[pltpu.VMEM((1, 4, win, win), F32)],
    )(info, probes)
    light_cross = to_cross(light_cross)
    light_near = to_near(light_near)
    ordered = kernel_call(order_kernel, [shape(count, win, win)], [VM] * 3)(
        amplitudes, pick, pick_back
    )

    near_half, cross_half, cross_outer = kernel_call(
        widen_kernel, [wide] * 2 + [outer], [VM] * 4
    )(info, close, specimen, far)
    cross_rows = (cross_inner, to_cross(cross_outer))
    near_rows = to_near(near_half)

    close, far = kernel_call(
        light_fold_kernel, [shape(1, tile, side)] * 2, [VM] * 4
    )(info, light_mid, light_near, light_cross)
    from_close, from_far = to_sides(close, far)
    light_near, light_cross, found = kernel_call(
        light_sum_kernel, [shape(half, 2 * side)] * 2 + [shape(8, LANES)], [VM] * 5
    )(info, close, far, from_close, from_far)
    peak = largest_of(found, ("col", "row"))

    for step in range(ITERS):
        first, last = step == 0, step + 1 == ITERS
        crossing = cross_rows if first else (cross_rows,)
        grad_near, *grad_cross, mid_near, mid_cross = kernel_call(
            functools.partial(gradient_kernel, first=first, last=last),
            [wide] + ([inner, outer] if last else [wide]) + [wide] * 2,
            [VM] * (9 + first),
            flops=count * 8 * 2 * win * 3 * win * win,
            scratch=[pltpu.VMEM((2, 4, win, win), F32)] * 2,
            grant=24,
        )(
            info, near_rows, *crossing, near_half, cross_half, probes, ordered,
            forward, backward,
        )
        sent_cross = to_cross(grad_cross[-1])
        if last:
            sent_inner = to_cross(grad_cross[0])
        sent_near = to_near(grad_near)
        if step + 1 < ITERS:
            halves = []
            for mid, sent, light, old in (
                (mid_cross, sent_cross, light_cross, cross_half),
                (mid_near, sent_near, light_near, near_half),
            ):
                close, far = kernel_call(fold_kernel, [strip] * 2, [VM] * 3)(info, mid, sent)
                from_close, from_far = to_sides(close, far)
                halves.append(
                    kernel_call(update_kernel, [wide], [VM] * 8)(
                        info, close, far, from_close, from_far, light, peak, old
                    )
                )
            cross_half, near_half = halves
            cross_rows = to_cross(cross_half)
            near_rows = to_near(near_half)
        else:
            operands = []
            for mid, sent, add, light, old in (
                (mid_near, sent_near, sent_near, light_near, near_half),
                (mid_cross, sent_cross, sent_inner, light_cross, cross_half),
            ):
                close, far = kernel_call(fold_last_kernel, [band] * 2, [VM] * 3)(info, mid, sent)
                from_close, from_far = to_sides(close, far)
                operands += [mid, add, from_close, from_far, light, old]
            return kernel_call(
                finish_kernel, [shape(2, tile, tile)], [VM] * 14
            )(info, *operands, peak)


def solution(mesh):
    return jax.shard_map(
        steps,
        mesh=mesh,
        in_specs=(
            P(None, "row", "col"),
            P(),
            P("row", "col", None, None),
            P("row", "col", None, None, None),
        ),
        out_specs=P(None, "row", "col"),
        check_vma=False,
    )
```

```python
import functools
import math

import jax
import jax.numpy as jnp
import numpy as np
from jax import lax
from jax.experimental import pallas as pl
from jax.experimental.pallas import tpu as pltpu
from jax.sharding import PartitionSpec as P


HALO = 128
ITERS = 2
LANES = 128
ODD, EVEN_COL, HAS_LEFT, HAS_RIGHT, FLAGS = 0, 1, 2, 3, 4

smooth_term = 0.25
ridge_share = 0.1

VM = pl.BlockSpec(memory_space=pltpu.VMEM)
SM = pl.BlockSpec(memory_space=pltpu.SMEM)
F32 = jnp.float32
BF16 = jnp.bfloat16


def shape(*dims):
    return jax.ShapeDtypeStruct(dims, F32)


def to_bf16(x):
    return np.asarray(x, np.float32).astype(BF16)


def split_table(table):
    high = to_bf16(table)
    low = to_bf16(table - high.astype(np.float64))
    return high, low


@functools.lru_cache
def dft_tables(length):
    half = length // 2
    n = np.arange(half)
    forward, backward = [], []
    for odd in (0, 1):
        turn = ((2 * n[:, None] + odd) * n[None, :]) % length
        angle = turn * (2.0 * math.pi / length)
        cos, sin = np.cos(angle) / math.sqrt(length), -np.sin(angle) / math.sqrt(length)
        form = np.block([[cos, -sin], [sin, cos]])
        forward.append(np.stack(split_table(form)))
        backward.append(np.stack(split_table(form.T)))
    place = np.zeros((length, length), np.float32)
    place[2 * n, n] = 1.0
    place[2 * n + 1, half + n] = 1.0
    pick = to_bf16(place)
    return np.stack(forward), np.stack(backward), pick, np.ascontiguousarray(pick.T)


def halves(x):
    high = x.astype(BF16)
    low = (x - high.astype(F32)).astype(BF16)
    return high, low


def left_product(table, x):
    high, low = halves(x)
    return jnp.dot(
        jnp.concatenate([table[0], table[1], table[0]], axis=1),
        jnp.concatenate([high, high, low], axis=0),
        preferred_element_type=F32,
    )


def right_product(x, table):
    high, low = halves(x)
    return jnp.dot(
        jnp.concatenate([high, low, high], axis=1),
        jnp.concatenate([table[0], table[0], table[1]], axis=0),
        preferred_element_type=F32,
    )


def window_masks(info, position, win):
    at = FLAGS + 2 * position
    low = lax.broadcasted_iota(jnp.int32, (win, win), 0) >= info[at : at + 1, :]
    near = lax.broadcasted_iota(jnp.int32, (win, win), 1) >= info[at + 1 : at + 2, :]
    return low, near


def flag(info, index):
    return info[index : index + 1, :] > 0


def roll_kernel(corners, probe, rolled):
    win = probe.shape[1]
    for position in range(rolled.shape[0]):
        row = lax.rem(corners[2 * position], win)
        column = lax.rem(corners[2 * position + 1], win)
        for plane in (0, 1):
            rolled[position, plane] = pltpu.roll(
                pltpu.roll(probe[plane], column, 1), row, 0
            )


def spread(piece, low, near, quadrants, first):
    above = jnp.where(low, piece, 0.0)
    below = jnp.where(low, 0.0, piece)
    parts = (
        jnp.where(near, above, 0.0), jnp.where(near, 0.0, above),
        jnp.where(near, below, 0.0), jnp.where(near, 0.0, below),
    )
    for index, part in enumerate(parts):
        quadrants[index] = part if first else quadrants[index] + part


def load_side(ref, plane, left, win):
    if not isinstance(ref, tuple):
        return ref[plane, :, left * win : (left + 1) * win]
    packed, outer = ref
    half = win - HALO
    width = packed.shape[2] // 2
    inner = packed[1, :, plane * width : (plane + 1) * width]
    if left:
        return jnp.concatenate([inner[:, half:], outer[plane, :, HALO:]], axis=1)
    return jnp.concatenate([outer[plane, :, :HALO], inner[:, :half]], axis=1)


def store_side(ref, plane, rows, left, value):
    win = value.shape[1]
    if not isinstance(ref, tuple):
        ref[plane, rows, left * win : (left + 1) * win] = value
        return
    inner, outer = ref
    half = win - HALO
    if left:
        inner[plane, rows, half:] = value[:, :half]
        outer[plane, rows, HALO:] = value[:, half:]
    else:
        outer[plane, rows, :HALO] = value[:, :HALO]
        inner[plane, rows, :half] = value[:, HALO:]


def gradient_kernel(*refs, first, last):
    refs = list(refs)
    if first:
        refs[2:4] = [tuple(refs[2:4])]
    if last:
        refs[10:12] = [tuple(refs[10:12])]
    gradient_body(*refs)


def gradient_body(
    info, near_rows, cross_rows, near_half, cross_half, probe, amplitude, forward, backward,
    grad_near, grad_cross, mid_near, mid_cross, area, total,
):
    count, win, _ = amplitude.shape
    half = win // 2
    odd_row = flag(info, ODD)
    for plane in (0, 1):
        for left in (0, 1):
            parts = [
                load_side(ref, plane, left, win)
                for ref in (near_rows, near_half, cross_half, cross_rows)
            ]
            for index in range(4):
                rows = slice((index % 2) * half, (index % 2 + 1) * half)
                area[plane, 2 * (index // 2) + left, rows] = jnp.where(
                    odd_row, parts[index], parts[3 - index]
                )

    def patch(plane, low, near):
        first, second, third, fourth = [area[plane, k] for k in range(4)]
        return jnp.where(
            near, jnp.where(low, first, third), jnp.where(low, second, fourth)
        )

    for position in range(count):
        low, near = window_masks(info, position, win)
        patch_real = patch(0, low, near)
        patch_imag = patch(1, low, near)
        probe_real, probe_imag = probe[position, 0], probe[position, 1]
        real = probe_real * patch_real - probe_imag * patch_imag
        imag = probe_real * patch_imag + probe_imag * patch_real
        summed = jnp.concatenate([real[:half] + real[half:], imag[:half] + imag[half:]], axis=0)
        differ = jnp.concatenate([real[:half] - real[half:], imag[:half] - imag[half:]], axis=0)
        even = left_product(forward[0], summed)
        odd = left_product(forward[1], differ)
        real = jnp.concatenate([even[:half], odd[:half]], axis=0)
        imag = jnp.concatenate([even[half:], odd[half:]], axis=0)
        summed = jnp.concatenate(
            [real[:, :half] + real[:, half:], imag[:, :half] + imag[:, half:]], axis=1
        )
        differ = jnp.concatenate(
            [real[:, :half] - real[:, half:], imag[:, :half] - imag[:, half:]], axis=1
        )
        even = right_product(summed, backward[0])
        odd = right_product(differ, backward[1])
        even_real, even_imag = even[:, :half], even[:, half:]
        odd_real, odd_imag = odd[:, :half], odd[:, half:]
        amp = amplitude[position]
        even_factor = 1.0 - amp[:, :half] * lax.rsqrt(
            even_real * even_real + even_imag * even_imag + smooth_term
        )
        odd_factor = 1.0 - amp[:, half:] * lax.rsqrt(
            odd_real * odd_real + odd_imag * odd_imag + smooth_term
        )
        even = jnp.concatenate([even_factor * even_real, even_factor * even_imag], axis=1)
        odd = jnp.concatenate([odd_factor * odd_real, odd_factor * odd_imag], axis=1)
        even_back = right_product(even, forward[0])
        odd_back = right_product(odd, forward[1])
        summed, differ = even_back + odd_back, even_back - odd_back
        real = jnp.concatenate([summed[:, :half], differ[:, :half]], axis=1)
        imag = jnp.concatenate([summed[:, half:], differ[:, half:]], axis=1)
        even = left_product(backward[0], jnp.concatenate([real[:half], imag[:half]], axis=0))
        odd = left_product(backward[1], jnp.concatenate([real[half:], imag[half:]], axis=0))
        summed, differ = even + odd, even - odd
        real = jnp.concatenate([summed[:half], differ[:half]], axis=0)
        imag = jnp.concatenate([summed[half:], differ[half:]], axis=0)
        for plane, piece in (
            (0, probe_real * real + probe_imag * imag),
            (1, probe_real * imag - probe_imag * real),
        ):
            spread(piece, low, near, total.at[plane], position == 0)
    whole = slice(None)
    for plane in (0, 1):
        by_halves(
            odd_row, total, plane,
            [(out, whole) for out in (grad_near, mid_near, mid_cross, grad_cross)],
        )


def by_halves(odd_row, total, plane, outs):
    half = total.shape[2] // 2
    for left in (0, 1):
        parts = [
            total[plane, 2 * (k // 2) + left, (k % 2) * half : (k % 2 + 1) * half]
            for k in range(4)
        ]
        for index, (out, rows) in enumerate(outs):
            store_side(
                out, plane, rows, left, jnp.where(odd_row, parts[index], parts[3 - index])
            )


def light_kernel(info, probe, specimen, light_near, light_mid, message, total):
    odd_row = flag(info, ODD)
    edge, tile = message.shape[1], specimen.shape[2]
    for plane in (0, 1):
        message[1, :, plane * tile : (plane + 1) * tile] = jnp.where(
            odd_row, specimen[plane, edge:], specimen[plane, :edge]
        )
    win = probe.shape[2]
    half = win // 2
    for position in range(probe.shape[0]):
        low, near = window_masks(info, position, win)
        real, imag = probe[position, 0], probe[position, 1]
        spread(real * real + imag * imag, low, near, total.at[0], position == 0)
    whole = slice(None)
    by_halves(
        flag(info, ODD), total, 0,
        (
            (light_near, whole), (light_mid, slice(0, half)),
            (light_mid, slice(half, win)), (message, whole),
        ),
    )


def light_fold_kernel(info, mid, sent_near, sent_cross, close, far):
    even_col = flag(info, EVEN_COL)
    half, side = sent_near.shape[1], close.shape[2]
    for rows, sent in ((slice(0, half), sent_near), (slice(half, None), sent_cross)):
        block = mid[0, rows] + sent[0]
        close[0, rows], far[0, rows] = by_sides(even_col, block[:, :side], block[:, side:])


def light_sum_kernel(
    info, close, far, from_close, from_far, light_near, light_cross, largest
):
    side = close.shape[2]
    half = light_near.shape[0]
    right, left = by_sides(
        flag(info, EVEN_COL), far[0] + from_far[0], close[0] + from_close[0]
    )
    for out, rows in ((light_near, slice(0, half)), (light_cross, slice(half, None))):
        out[:, :side] = left[rows]
        out[:, side:] = right[rows]
    found = None
    for best in (left[:, HALO:], right[:, : side - HALO]):
        for row in range(0, best.shape[0], 8):
            for lane in range(0, best.shape[1], LANES):
                block = best[row : row + 8, lane : lane + LANES]
                found = block if found is None else jnp.maximum(found, block)
    largest[...] = found


def thirds(x):
    high = x.astype(BF16)
    rest = x - high.astype(F32)
    mid = rest.astype(BF16)
    return high, mid, (rest - mid.astype(F32)).astype(BF16)


def order_kernel(amplitude, pick, pick_back, ordered):
    rows = jnp.concatenate([pick_back[...]] * 3, axis=1)
    columns = jnp.concatenate([pick[...]] * 3, axis=0)
    for position in range(ordered.shape[0]):
        block = jnp.dot(
            rows,
            jnp.concatenate(thirds(amplitude[0, 0, position]), axis=0),
            preferred_element_type=F32,
        )
        ordered[position] = jnp.dot(
            jnp.concatenate(thirds(block), axis=1), columns, preferred_element_type=F32
        )


def by_sides(even_col, head, tail):
    even_col = even_col[:, : head.shape[-1]]
    return jnp.where(even_col, tail, head), jnp.where(even_col, head, tail)


def edges_kernel(specimen, close, far):
    even_col = lax.axis_index("col") % 2 == 0
    for plane in (0, 1):
        head, tail = specimen[plane, :, :HALO], specimen[plane, :, specimen.shape[2] - HALO :]
        close[plane] = jnp.where(even_col, tail, head)
        far[plane] = jnp.where(even_col, head, tail)


def widen_kernel(info, close, specimen, far, near_half, cross_half, cross_outer):
    odd_row, even_col = flag(info, ODD), flag(info, EVEN_COL)
    half, tile = near_half.shape[1], specimen.shape[2]
    for plane in (0, 1):
        after, before = by_sides(even_col, far[plane], close[plane])
        for source, lanes in (
            (before, slice(0, HALO)),
            (specimen[plane], slice(HALO, HALO + tile)),
            (after, slice(HALO + tile, None)),
        ):
            odd = odd_row[:, : source.shape[1]]
            top, bottom = source[:half], source[half:]
            near_half[plane, :, lanes] = jnp.where(odd, top, bottom)
            cross_half[plane, :, lanes] = jnp.where(odd, bottom, top)
        cross_outer[plane, :, :HALO] = cross_half[plane, :, :HALO]
        cross_outer[plane, :, HALO:] = cross_half[plane, :, HALO + tile :]


def fold_kernel(info, mid, sent, close, far):
    even_col = flag(info, EVEN_COL)
    side = close.shape[2]
    for plane in (0, 1):
        block = mid[plane] + sent[plane]
        close[plane], far[plane] = by_sides(even_col, block[:, :side], block[:, side:])


def fold_last_kernel(info, mid, sent, close, far):
    even_col = flag(info, EVEN_COL)
    for plane in (0, 1):
        head = mid[plane, :, :HALO] + sent[plane, :, :HALO]
        tail = mid[plane, :, mid.shape[2] - HALO :] + sent[plane, :, sent.shape[2] - HALO :]
        close[plane], far[plane] = by_sides(even_col, head, tail)


def update_kernel(info, close, far, from_close, from_far, light, peak, old, new):
    even_col = flag(info, EVEN_COL)
    side = close.shape[2]
    most = ridge_share * jnp.max(peak[...])
    lane = lax.broadcasted_iota(jnp.int32, (1, side), 1)
    bounds = (
        ((lane >= HALO) | flag(info, HAS_LEFT), slice(0, side)),
        ((lane < side - HALO) | flag(info, HAS_RIGHT), slice(side, None)),
    )
    scales = [1.0 / (light[:, lanes] + most) for _, lanes in bounds]
    for plane in (0, 1):
        right, left = by_sides(
            even_col, far[plane] + from_far[plane], close[plane] + from_close[plane]
        )
        for gradient, scale, (inside, lanes) in zip((left, right), scales, bounds):
            new[plane, :, lanes] = jnp.where(
                inside, old[plane, :, lanes] - gradient * scale, 0.0
            )


def finish_kernel(info, *refs):
    *halves, peak, out = refs
    odd_row, even_col = flag(info, ODD), flag(info, EVEN_COL)
    most = ridge_share * jnp.max(peak[...])
    half, tile = out.shape[1] // 2, out.shape[2]
    inner = slice(HALO, HALO + tile)
    for plane in (0, 1):
        news = []
        for mid, add, from_close, from_far, light, old in (halves[:6], halves[6:]):
            right, left = by_sides(even_col, from_far[plane], from_close[plane])
            sent = [left, right]
            if tile > 2 * HALO:
                sent.insert(1, jnp.zeros((half, tile - 2 * HALO), F32))
            add = add[plane] if add.shape[2] == tile else add[plane, :, inner]
            gradient = mid[plane, :, inner] + add + jnp.concatenate(sent, axis=1)
            news.append(old[plane, :, inner] - gradient / (light[:, inner] + most))
        out[plane, :half] = jnp.where(odd_row, news[0], news[1])
        out[plane, half:] = jnp.where(odd_row, news[1], news[0])


def kernel_call(body, outs, specs, flops=0, scratch=(), grant=8):
    moved = 4 * sum(math.prod(out.shape) for out in outs)
    single = len(outs) == 1
    return pl.pallas_call(
        body,
        out_shape=outs[0] if single else outs,
        in_specs=specs,
        out_specs=VM if single else (VM,) * len(outs),
        scratch_shapes=list(scratch),
        compiler_params=pltpu.CompilerParams(vmem_limit_bytes=grant * 1024 * 1024),
        cost_estimate=pl.CostEstimate(
            flops=flops, bytes_accessed=3 * moved, transcendentals=0
        ),
    )


def swapped(block, axis, first):
    count = lax.axis_size(axis)
    route = []
    for i in range(first, count - 1, 2):
        route += [(i, i + 1), (i + 1, i)]
    return lax.ppermute(block, axis, route)


def to_cross(block):
    return swapped(block, "row", 1)


def to_near(block):
    return swapped(block, "row", 0)


def to_sides(close, far):
    close = swapped(close, "col", 0)
    far = swapped(far, "col", 1)
    return close, far


def largest_of(block, axis, reaches):
    count = lax.axis_size(axis)
    for reach in reaches:
        if count & (count - 1) == 0:
            route = [(i, i ^ reach) for i in range(count)]
        else:
            route = [(i, (i + reach) % count) for i in range(count)]
        block = jnp.maximum(block, lax.ppermute(block, axis, route))
    return block


def doublings(axis):
    return [2**k for k in range((lax.axis_size(axis) - 1).bit_length())]


def steps(specimen, probe_field, offsets, amplitudes):
    tile = specimen.shape[1]
    win = probe_field.shape[1]
    side = tile // 2 + HALO
    half = tile // 2
    count = offsets.shape[2]
    forward, backward, pick, pick_back = [jnp.asarray(t) for t in dft_tables(win)]
    row, col = lax.axis_index("row"), lax.axis_index("col")
    odd = row % 2
    corners = offsets.reshape(-1) + HALO
    flags = jnp.stack([odd, (col + 1) % 2, col > 0, col < lax.axis_size("col") - 1]).astype(jnp.int32)
    info = jnp.broadcast_to(
        jnp.concatenate([flags, corners])[:, None], (FLAGS + 2 * count, win)
    )
    band, wide, strip = shape(2, half, HALO), shape(2, half, 2 * side), shape(2, half, side)
    inner, outer = shape(2, half, tile), shape(2, half, 2 * HALO)

    close, far = kernel_call(edges_kernel, [shape(2, tile, HALO)] * 2, [VM])(
        specimen
    )
    close, far = to_sides(close, far)

    probes = kernel_call(roll_kernel, [shape(count, 2, win, win)], [SM, VM])(corners, probe_field)
    light_band = shape(1, half, 2 * side)
    light_near, light_mid, message = kernel_call(
        light_kernel,
        [light_band, shape(1, tile, 2 * side), wide],
        [VM] * 3,
        scratch=[pltpu.VMEM((1, 4, win, win), F32)],
    )(info, probes, specimen)
    message = to_cross(message)
    light_near = to_near(light_near)
    ordered = kernel_call(order_kernel, [shape(count, win, win)], [VM] * 3)(
        amplitudes, pick, pick_back
    )

    near_half, cross_half, cross_outer = kernel_call(
        widen_kernel, [wide] * 2 + [outer], [VM] * 4
    )(info, close, specimen, far)
    cross_rows = (message, to_cross(cross_outer))
    near_rows = to_near(near_half)

    close, far = kernel_call(
        light_fold_kernel, [shape(1, tile, side)] * 2, [VM] * 4
    )(info, light_mid, light_near, message)
    from_close, from_far = to_sides(close, far)
    light_near, light_cross, found = kernel_call(
        light_sum_kernel, [shape(half, 2 * side)] * 2 + [shape(8, LANES)], [VM] * 5
    )(info, close, far, from_close, from_far)
    found = largest_of(found, "col", doublings("col"))
    found = largest_of(found, "row", doublings("row")[:0:-1])
    peak = None

    for step in range(ITERS):
        first, last = step == 0, step + 1 == ITERS
        crossing = cross_rows if first else (cross_rows,)
        grad_near, *grad_cross, mid_near, mid_cross = kernel_call(
            functools.partial(gradient_kernel, first=first, last=last),
            [wide] + ([inner, outer] if last else [wide]) + [wide] * 2,
            [VM] * (9 + first),
            flops=count * 8 * 2 * win * 3 * win * win,
            scratch=[pltpu.VMEM((2, 4, win, win), F32)] * 2,
            grant=24,
        )(
            info, near_rows, *crossing, near_half, cross_half, probes, ordered,
            forward, backward,
        )
        sent_cross = to_cross(grad_cross[-1])
        if last:
            sent_inner = to_cross(grad_cross[0])
        sent_near = to_near(grad_near)
        if step + 1 < ITERS:
            halves = []
            for mid, sent, light, old in (
                (mid_cross, sent_cross, light_cross, cross_half),
                (mid_near, sent_near, light_near, near_half),
            ):
                close, far = kernel_call(fold_kernel, [strip] * 2, [VM] * 3)(info, mid, sent)
                from_close, from_far = to_sides(close, far)
                if peak is None:
                    found, from_close = lax.optimization_barrier((found, from_close))
                    peak = largest_of(found, "row", doublings("row")[:1])
                halves.append(
                    kernel_call(update_kernel, [wide], [VM] * 8)(
                        info, close, far, from_close, from_far, light, peak, old
                    )
                )
            cross_half, near_half = halves
            cross_rows = to_cross(cross_half)
            near_rows = to_near(near_half)
        else:
            operands = []
            for mid, sent, add, light, old in (
                (mid_near, sent_near, sent_near, light_near, near_half),
                (mid_cross, sent_cross, sent_inner, light_cross, cross_half),
            ):
                close, far = kernel_call(fold_last_kernel, [band] * 2, [VM] * 3)(info, mid, sent)
                from_close, from_far = to_sides(close, far)
                operands += [mid, add, from_close, from_far, light, old]
            return kernel_call(
                finish_kernel, [shape(2, tile, tile)], [VM] * 14
            )(info, *operands, peak)


def solution(mesh):
    return jax.shard_map(
        steps,
        mesh=mesh,
        in_specs=(
            P(None, "row", "col"),
            P(),
            P("row", "col", None, None),
            P("row", "col", None, None, None),
        ),
        out_specs=P(None, "row", "col"),
        check_vma=False,
    )
```

```python
import functools
import math

import jax
import jax.numpy as jnp
import numpy as np
from jax import lax
from jax.experimental import pallas as pl
from jax.experimental.pallas import tpu as pltpu
from jax.sharding import PartitionSpec as P


HALO = 128
ITERS = 2
LANES = 128
ODD, EVEN_COL, HAS_LEFT, HAS_RIGHT, FLAGS = 0, 1, 2, 3, 4

smooth_term = 0.25
ridge_share = 0.1

VM = pl.BlockSpec(memory_space=pltpu.VMEM)
SM = pl.BlockSpec(memory_space=pltpu.SMEM)
F32 = jnp.float32
BF16 = jnp.bfloat16


def shape(*dims):
    return jax.ShapeDtypeStruct(dims, F32)


def to_bf16(x):
    return np.asarray(x, np.float32).astype(BF16)


def split_table(table):
    high = to_bf16(table)
    low = to_bf16(table - high.astype(np.float64))
    return high, low


@functools.lru_cache
def dft_tables(length):
    half = length // 2
    n = np.arange(half)
    forward, backward = [], []
    for odd in (0, 1):
        turn = ((2 * n[:, None] + odd) * n[None, :]) % length
        angle = turn * (2.0 * math.pi / length)
        cos, sin = np.cos(angle) / math.sqrt(length), -np.sin(angle) / math.sqrt(length)
        form = np.block([[cos, -sin], [sin, cos]])
        forward.append(np.stack(split_table(form)))
        backward.append(np.stack(split_table(form.T)))
    place = np.zeros((length, length), np.float32)
    place[2 * n, n] = 1.0
    place[2 * n + 1, half + n] = 1.0
    pick = to_bf16(place)
    return np.stack(forward), np.stack(backward), pick, np.ascontiguousarray(pick.T)


def halves(x):
    high = x.astype(BF16)
    low = (x - high.astype(F32)).astype(BF16)
    return high, low


def left_product(table, x):
    high, low = halves(x)
    return jnp.dot(
        jnp.concatenate([table[0], table[1], table[0]], axis=1),
        jnp.concatenate([high, high, low], axis=0),
        preferred_element_type=F32,
    )


def right_product(x, table):
    high, low = halves(x)
    return jnp.dot(
        jnp.concatenate([high, low, high], axis=1),
        jnp.concatenate([table[0], table[0], table[1]], axis=0),
        preferred_element_type=F32,
    )


def window_masks(info, position, win):
    at = FLAGS + 2 * position
    low = lax.broadcasted_iota(jnp.int32, (win, win), 0) >= info[at : at + 1, :]
    near = lax.broadcasted_iota(jnp.int32, (win, win), 1) >= info[at + 1 : at + 2, :]
    return low, near


def flag(info, index):
    return info[index : index + 1, :] > 0


def roll_kernel(corners, probe, rolled):
    win = probe.shape[1]
    for position in range(rolled.shape[0]):
        row = lax.rem(corners[2 * position], win)
        column = lax.rem(corners[2 * position + 1], win)
        for plane in (0, 1):
            rolled[position, plane] = pltpu.roll(
                pltpu.roll(probe[plane], column, 1), row, 0
            )


def spread(piece, low, near, quadrants, first):
    above = jnp.where(low, piece, 0.0)
    below = jnp.where(low, 0.0, piece)
    parts = (
        jnp.where(near, above, 0.0), jnp.where(near, 0.0, above),
        jnp.where(near, below, 0.0), jnp.where(near, 0.0, below),
    )
    for index, part in enumerate(parts):
        quadrants[index] = part if first else quadrants[index] + part


def load_side(ref, plane, left, win):
    if not isinstance(ref, tuple):
        return ref[plane, :, left * win : (left + 1) * win]
    inner, outer = ref
    half = win - HALO
    if left:
        return jnp.concatenate([inner[plane, :, half:], outer[plane, :, HALO:]], axis=1)
    return jnp.concatenate([outer[plane, :, :HALO], inner[plane, :, :half]], axis=1)


def store_side(ref, plane, rows, left, value):
    win = value.shape[1]
    if not isinstance(ref, tuple):
        ref[plane, rows, left * win : (left + 1) * win] = value
        return
    inner, outer = ref
    half = win - HALO
    if left:
        inner[plane, rows, half:] = value[:, :half]
        outer[plane, rows, HALO:] = value[:, half:]
    else:
        outer[plane, rows, :HALO] = value[:, :HALO]
        inner[plane, rows, :half] = value[:, HALO:]


def gradient_kernel(*refs, first, last):
    refs = list(refs)
    if first:
        refs[2:4] = [tuple(refs[2:4])]
    if last:
        refs[10:12] = [tuple(refs[10:12])]
    gradient_body(*refs)


def gradient_body(
    info, near_rows, cross_rows, near_half, cross_half, probe, amplitude, forward, backward,
    grad_near, grad_cross, mid_near, mid_cross, area, total,
):
    count, win, _ = amplitude.shape
    half = win // 2
    odd_row = flag(info, ODD)
    for plane in (0, 1):
        for left in (0, 1):
            parts = [
                load_side(ref, plane, left, win)
                for ref in (near_rows, near_half, cross_half, cross_rows)
            ]
            for index in range(4):
                rows = slice((index % 2) * half, (index % 2 + 1) * half)
                area[plane, 2 * (index // 2) + left, rows] = jnp.where(
                    odd_row, parts[index], parts[3 - index]
                )

    def patch(plane, low, near):
        first, second, third, fourth = [area[plane, k] for k in range(4)]
        return jnp.where(
            near, jnp.where(low, first, third), jnp.where(low, second, fourth)
        )

    for position in range(count):
        low, near = window_masks(info, position, win)
        patch_real = patch(0, low, near)
        patch_imag = patch(1, low, near)
        probe_real, probe_imag = probe[position, 0], probe[position, 1]
        real = probe_real * patch_real - probe_imag * patch_imag
        imag = probe_real * patch_imag + probe_imag * patch_real
        summed = jnp.concatenate([real[:half] + real[half:], imag[:half] + imag[half:]], axis=0)
        differ = jnp.concatenate([real[:half] - real[half:], imag[:half] - imag[half:]], axis=0)
        even = left_product(forward[0], summed)
        odd = left_product(forward[1], differ)
        real = jnp.concatenate([even[:half], odd[:half]], axis=0)
        imag = jnp.concatenate([even[half:], odd[half:]], axis=0)
        summed = jnp.concatenate(
            [real[:, :half] + real[:, half:], imag[:, :half] + imag[:, half:]], axis=1
        )
        differ = jnp.concatenate(
            [real[:, :half] - real[:, half:], imag[:, :half] - imag[:, half:]], axis=1
        )
        even = right_product(summed, backward[0])
        odd = right_product(differ, backward[1])
        even_real, even_imag = even[:, :half], even[:, half:]
        odd_real, odd_imag = odd[:, :half], odd[:, half:]
        amp = amplitude[position]
        even_factor = 1.0 - amp[:, :half] * lax.rsqrt(
            even_real * even_real + even_imag * even_imag + smooth_term
        )
        odd_factor = 1.0 - amp[:, half:] * lax.rsqrt(
            odd_real * odd_real + odd_imag * odd_imag + smooth_term
        )
        even = jnp.concatenate([even_factor * even_real, even_factor * even_imag], axis=1)
        odd = jnp.concatenate([odd_factor * odd_real, odd_factor * odd_imag], axis=1)
        even_back = right_product(even, forward[0])
        odd_back = right_product(odd, forward[1])
        summed, differ = even_back + odd_back, even_back - odd_back
        real = jnp.concatenate([summed[:, :half], differ[:, :half]], axis=1)
        imag = jnp.concatenate([summed[:, half:], differ[:, half:]], axis=1)
        even = left_product(backward[0], jnp.concatenate([real[:half], imag[:half]], axis=0))
        odd = left_product(backward[1], jnp.concatenate([real[half:], imag[half:]], axis=0))
        summed, differ = even + odd, even - odd
        real = jnp.concatenate([summed[:half], differ[:half]], axis=0)
        imag = jnp.concatenate([summed[half:], differ[half:]], axis=0)
        for plane, piece in (
            (0, probe_real * real + probe_imag * imag),
            (1, probe_real * imag - probe_imag * real),
        ):
            spread(piece, low, near, total.at[plane], position == 0)
    whole = slice(None)
    for plane in (0, 1):
        by_halves(
            odd_row, total, plane,
            [(out, whole) for out in (grad_near, mid_near, mid_cross, grad_cross)],
        )


def by_halves(odd_row, total, plane, outs):
    half = total.shape[2] // 2
    for left in (0, 1):
        parts = [
            total[plane, 2 * (k // 2) + left, (k % 2) * half : (k % 2 + 1) * half]
            for k in range(4)
        ]
        for index, (out, rows) in enumerate(outs):
            store_side(
                out, plane, rows, left, jnp.where(odd_row, parts[index], parts[3 - index])
            )


def light_kernel(info, probe, light_near, light_mid, light_cross, total):
    win = probe.shape[2]
    half = win // 2
    for position in range(probe.shape[0]):
        low, near = window_masks(info, position, win)
        real, imag = probe[position, 0], probe[position, 1]
        spread(real * real + imag * imag, low, near, total.at[0], position == 0)
    whole = slice(None)
    by_halves(
        flag(info, ODD), total, 0,
        (
            (light_near, whole), (light_mid, slice(0, half)),
            (light_mid, slice(half, win)), (light_cross, whole),
        ),
    )


def light_fold_kernel(info, mid, sent_near, sent_cross, close, far):
    even_col = flag(info, EVEN_COL)
    half, side = sent_near.shape[1], close.shape[2]
    for rows, sent in ((slice(0, half), sent_near), (slice(half, None), sent_cross)):
        block = mid[0, rows] + sent[0]
        close[0, rows], far[0, rows] = by_sides(even_col, block[:, :side], block[:, side:])


def light_sum_kernel(
    info, close, far, from_close, from_far, light_near, light_cross, largest
):
    side = close.shape[2]
    half = light_near.shape[0]
    right, left = by_sides(
        flag(info, EVEN_COL), far[0] + from_far[0], close[0] + from_close[0]
    )
    for out, rows in ((light_near, slice(0, half)), (light_cross, slice(half, None))):
        out[:, :side] = left[rows]
        out[:, side:] = right[rows]
    found = None
    for best in (left[:, HALO:], right[:, : side - HALO]):
        for row in range(0, best.shape[0], 8):
            for lane in range(0, best.shape[1], LANES):
                block = best[row : row + 8, lane : lane + LANES]
                found = block if found is None else jnp.maximum(found, block)
    largest[...] = found


def thirds(x):
    high = x.astype(BF16)
    rest = x - high.astype(F32)
    mid = rest.astype(BF16)
    return high, mid, (rest - mid.astype(F32)).astype(BF16)


def order_kernel(amplitude, pick, pick_back, ordered):
    rows = jnp.concatenate([pick_back[...]] * 3, axis=1)
    columns = jnp.concatenate([pick[...]] * 3, axis=0)
    for position in range(ordered.shape[0]):
        block = jnp.dot(
            rows,
            jnp.concatenate(thirds(amplitude[0, 0, position]), axis=0),
            preferred_element_type=F32,
        )
        ordered[position] = jnp.dot(
            jnp.concatenate(thirds(block), axis=1), columns, preferred_element_type=F32
        )


def by_sides(even_col, head, tail):
    even_col = even_col[:, : head.shape[-1]]
    return jnp.where(even_col, tail, head), jnp.where(even_col, head, tail)


def edges_kernel(specimen, close, far):
    even_col = lax.axis_index("col") % 2 == 0
    for plane in (0, 1):
        head, tail = specimen[plane, :, :HALO], specimen[plane, :, specimen.shape[2] - HALO :]
        close[plane] = jnp.where(even_col, tail, head)
        far[plane] = jnp.where(even_col, head, tail)


def center_kernel(info, specimen, cross):
    odd_row = flag(info, ODD)
    half = cross.shape[1]
    for plane in (0, 1):
        cross[plane] = jnp.where(odd_row, specimen[plane, half:], specimen[plane, :half])


def widen_kernel(info, close, specimen, far, near_half, cross_half, cross_outer):
    odd_row, even_col = flag(info, ODD), flag(info, EVEN_COL)
    half, tile = near_half.shape[1], specimen.shape[2]
    for plane in (0, 1):
        after, before = by_sides(even_col, far[plane], close[plane])
        for source, lanes in (
            (before, slice(0, HALO)),
            (specimen[plane], slice(HALO, HALO + tile)),
            (after, slice(HALO + tile, None)),
        ):
            odd = odd_row[:, : source.shape[1]]
            top, bottom = source[:half], source[half:]
            near_half[plane, :, lanes] = jnp.where(odd, top, bottom)
            cross_half[plane, :, lanes] = jnp.where(odd, bottom, top)
        cross_outer[plane, :, :HALO] = cross_half[plane, :, :HALO]
        cross_outer[plane, :, HALO:] = cross_half[plane, :, HALO + tile :]


def fold_kernel(info, mid, sent, close, far):
    even_col = flag(info, EVEN_COL)
    side = close.shape[2]
    for plane in (0, 1):
        block = mid[plane] + sent[plane]
        close[plane], far[plane] = by_sides(even_col, block[:, :side], block[:, side:])


def fold_last_kernel(info, mid, sent, close, far):
    even_col = flag(info, EVEN_COL)
    for plane in (0, 1):
        head = mid[plane, :, :HALO] + sent[plane, :, :HALO]
        tail = mid[plane, :, mid.shape[2] - HALO :] + sent[plane, :, sent.shape[2] - HALO :]
        close[plane], far[plane] = by_sides(even_col, head, tail)


def update_kernel(info, close, far, from_close, from_far, light, peak, old, new):
    even_col = flag(info, EVEN_COL)
    side = close.shape[2]
    most = ridge_share * jnp.max(peak[...])
    lane = lax.broadcasted_iota(jnp.int32, (1, side), 1)
    bounds = (
        ((lane >= HALO) | flag(info, HAS_LEFT), slice(0, side)),
        ((lane < side - HALO) | flag(info, HAS_RIGHT), slice(side, None)),
    )
    scales = [1.0 / (light[:, lanes] + most) for _, lanes in bounds]
    for plane in (0, 1):
        right, left = by_sides(
            even_col, far[plane] + from_far[plane], close[plane] + from_close[plane]
        )
        for gradient, scale, (inside, lanes) in zip((left, right), scales, bounds):
            new[plane, :, lanes] = jnp.where(
                inside, old[plane, :, lanes] - gradient * scale, 0.0
            )


def finish_kernel(info, *refs):
    *halves, peak, out = refs
    odd_row, even_col = flag(info, ODD), flag(info, EVEN_COL)
    most = ridge_share * jnp.max(peak[...])
    half, tile = out.shape[1] // 2, out.shape[2]
    inner = slice(HALO, HALO + tile)
    for plane in (0, 1):
        news = []
        for mid, add, from_close, from_far, light, old in (halves[:6], halves[6:]):
            right, left = by_sides(even_col, from_far[plane], from_close[plane])
            sent = [left, right]
            if tile > 2 * HALO:
                sent.insert(1, jnp.zeros((half, tile - 2 * HALO), F32))
            add = add[plane] if add.shape[2] == tile else add[plane, :, inner]
            gradient = mid[plane, :, inner] + add + jnp.concatenate(sent, axis=1)
            news.append(old[plane, :, inner] - gradient / (light[:, inner] + most))
        out[plane, :half] = jnp.where(odd_row, news[0], news[1])
        out[plane, half:] = jnp.where(odd_row, news[1], news[0])


def kernel_call(body, outs, specs, flops=0, scratch=(), grant=8):
    moved = 4 * sum(math.prod(out.shape) for out in outs)
    single = len(outs) == 1
    return pl.pallas_call(
        body,
        out_shape=outs[0] if single else outs,
        in_specs=specs,
        out_specs=VM if single else (VM,) * len(outs),
        scratch_shapes=list(scratch),
        compiler_params=pltpu.CompilerParams(vmem_limit_bytes=grant * 1024 * 1024),
        cost_estimate=pl.CostEstimate(
            flops=flops, bytes_accessed=3 * moved, transcendentals=0
        ),
    )


def swapped(block, axis, first):
    count = lax.axis_size(axis)
    route = []
    for i in range(first, count - 1, 2):
        route += [(i, i + 1), (i + 1, i)]
    return lax.ppermute(block, axis, route)


def to_cross(block):
    return swapped(block, "row", 1)


def to_near(block):
    return swapped(block, "row", 0)


def to_sides(close, far):
    close = swapped(close, "col", 0)
    far = swapped(far, "col", 1)
    return close, far


def largest_of(block, axis, reaches):
    count = lax.axis_size(axis)
    for reach in reaches:
        if count & (count - 1) == 0:
            route = [(i, i ^ reach) for i in range(count)]
        else:
            route = [(i, (i + reach) % count) for i in range(count)]
        block = jnp.maximum(block, lax.ppermute(block, axis, route))
    return block


def doublings(axis):
    return [2**k for k in range((lax.axis_size(axis) - 1).bit_length())]


def steps(specimen, probe_field, offsets, amplitudes):
    tile = specimen.shape[1]
    win = probe_field.shape[1]
    side = tile // 2 + HALO
    half = tile // 2
    count = offsets.shape[2]
    forward, backward, pick, pick_back = [jnp.asarray(t) for t in dft_tables(win)]
    row, col = lax.axis_index("row"), lax.axis_index("col")
    odd = row % 2
    corners = offsets.reshape(-1) + HALO
    flags = jnp.stack([odd, (col + 1) % 2, col > 0, col < lax.axis_size("col") - 1]).astype(jnp.int32)
    info = jnp.broadcast_to(
        jnp.concatenate([flags, corners])[:, None], (FLAGS + 2 * count, win)
    )
    band, wide, strip = shape(2, half, HALO), shape(2, half, 2 * side), shape(2, half, side)
    inner, outer = shape(2, half, tile), shape(2, half, 2 * HALO)

    close, far = kernel_call(edges_kernel, [shape(2, tile, HALO)] * 2, [VM])(
        specimen
    )
    close, far = to_sides(close, far)

    cross_inner = to_cross(kernel_call(center_kernel, [inner], [VM] * 2)(info, specimen))

    probes = kernel_call(roll_kernel, [shape(count, 2, win, win)], [SM, VM])(corners, probe_field)
    light_band = shape(1, half, 2 * side)
    light_near, light_mid, light_cross = kernel_call(
        light_kernel,
        [light_band, shape(1, tile, 2 * side), light_band],
        [VM] * 2,
        scratch=[pltpu.VMEM((1, 4, win, win), F32)],
    )(info, probes)
    light_cross = to_cross(light_cross)
    light_near = to_near(light_near)
    ordered = kernel_call(order_kernel, [shape(count, win, win)], [VM] * 3)(
        amplitudes, pick, pick_back
    )

    near_half, cross_half, cross_outer = kernel_call(
        widen_kernel, [wide] * 2 + [outer], [VM] * 4
    )(info, close, specimen, far)
    cross_rows = (cross_inner, to_cross(cross_outer))
    near_rows = to_near(near_half)

    close, far = kernel_call(
        light_fold_kernel, [shape(1, tile, side)] * 2, [VM] * 4
    )(info, light_mid, light_near, light_cross)
    from_close, from_far = to_sides(close, far)
    light_near, light_cross, found = kernel_call(
        light_sum_kernel, [shape(half, 2 * side)] * 2 + [shape(8, LANES)], [VM] * 5
    )(info, close, far, from_close, from_far)
    found = largest_of(found, "col", doublings("col"))
    found = largest_of(found, "row", doublings("row")[:0:-1])
    peak = None

    for step in range(ITERS):
        first, last = step == 0, step + 1 == ITERS
        crossing = cross_rows if first else (cross_rows,)
        grad_near, *grad_cross, mid_near, mid_cross = kernel_call(
            functools.partial(gradient_kernel, first=first, last=last),
            [wide] + ([inner, outer] if last else [wide]) + [wide] * 2,
            [VM] * (9 + first),
            flops=count * 8 * 2 * win * 3 * win * win,
            scratch=[pltpu.VMEM((2, 4, win, win), F32)] * 2,
            grant=24,
        )(
            info, near_rows, *crossing, near_half, cross_half, probes, ordered,
            forward, backward,
        )
        sent_cross = to_cross(grad_cross[-1])
        if last:
            sent_inner = to_cross(grad_cross[0])
        sent_near = to_near(grad_near)
        if step + 1 < ITERS:
            halves = []
            for mid, sent, light, old in (
                (mid_cross, sent_cross, light_cross, cross_half),
                (mid_near, sent_near, light_near, near_half),
            ):
                close, far = kernel_call(fold_kernel, [strip] * 2, [VM] * 3)(info, mid, sent)
                from_close, from_far = to_sides(close, far)
                if peak is None:
                    peak = largest_of(found, "row", doublings("row")[:1])
                halves.append(
                    kernel_call(update_kernel, [wide], [VM] * 8)(
                        info, close, far, from_close, from_far, light, peak, old
                    )
                )
            cross_half, near_half = halves
            cross_rows = to_cross(cross_half)
            near_rows = to_near(near_half)
        else:
            operands = []
            for mid, sent, add, light, old in (
                (mid_near, sent_near, sent_near, light_near, near_half),
                (mid_cross, sent_cross, sent_inner, light_cross, cross_half),
            ):
                close, far = kernel_call(fold_last_kernel, [band] * 2, [VM] * 3)(info, mid, sent)
                from_close, from_far = to_sides(close, far)
                operands += [mid, add, from_close, from_far, light, old]
            return kernel_call(
                finish_kernel, [shape(2, tile, tile)], [VM] * 14
            )(info, *operands, peak)


def solution(mesh):
    return jax.shard_map(
        steps,
        mesh=mesh,
        in_specs=(
            P(None, "row", "col"),
            P(),
            P("row", "col", None, None),
            P("row", "col", None, None, None),
        ),
        out_specs=P(None, "row", "col"),
        check_vma=False,
    )
```
